32 devices in a mesh: cuts: 4 (over y, x), det: 2 (over core), bank: 4 (over z).
Axes of the slice: x: 2, y: 2, z: 4, core: 2. Of those that a mesh axis runs over, the one named last changes fastest.
Arguments:
- strain: bfloat16 [4, 2, 6144], P('cuts', 'det'), may hold values from -6 to 6
- filters: bfloat16 [16, 256, 2048], P(('bank', 'cuts')), parts along dimension 0, may hold values from -0.125 to 0.125
- recon_weights: bfloat16 [16, 128, 256], P(('bank', 'cuts')), parts along dimension 0, may hold values from -0.1875 to 0.1875
- row_spans: int32 [512], P('bank'), parts along dimension 0, may hold values from 1 to 4
- slice_rates: int32 [4], replicated, may hold values from 1 to 8, as said below
- delays: int32 [64, 2], replicated, may hold values from 0 to 47
- antenna: float32 [64, 2], replicated, may hold values from 0.2 to 1
Outputs:
- peak_amplitude: float32 [512, 4096], P(('bank', 'cuts', 'det')), parts along dimension 0
The draws below stay inside these ranges and needn't reach their ends.
There are 4 independent parts, one for each index of `bank`. The reference program is written for one: setup_inputs(seed, part) draws one part's arguments, and reference() takes and returns one part's arrays. A program takes and returns all parts, laid end to end along the dimension named above; an argument that names none is the same for every part. Nothing has to cross between parts.
Inputs may be any that keep to these rules, and one draw needn't show every extreme that they name: `slice_rates`: every entry is a power of two; entries never fall along the slices; the first is 1 and the last is 8.
All inputs are finite; a program needn't handle non-finite values.
Results may differ from the reference program's by a relative error of at most 0.0014.
Values sent between devices are 32-bit elements; how exact they have to be, the bound alone decides.
A program may use at most 64 MiB of HBM per device.

```python
import jax
import jax.numpy as jnp
from jax import lax

WIN = 4096
TAPS = 2048
BASES = 256
FMAX = 8
DIRS = 64
MAXD = 48
SLICES = 4
DETS = 2
ROWS = 128
N_CUTS = 4


def draw_slice_rates(key, part):
    top_level = FMAX.bit_length() - 1
    levels = jnp.sort(jax.random.randint(key, (SLICES,), 0, top_level + 1))
    levels = levels.at[0].set(0).at[SLICES - 1].set(top_level)
    return jnp.left_shift(jnp.ones((SLICES,), jnp.int32), levels).astype(jnp.int32)


def place_ends(values, stream_key, least, high):
    extent = values.shape
    index_at = [jax.random.randint(jax.random.fold_in(stream_key, axis), (), 0, extent[axis]) for axis in range(len(extent))]
    values = values.at[tuple(index_at)].set(least)
    longest = extent.index(max(extent))
    index_at[longest] = (index_at[longest] + 1) % extent[longest]
    return values.at[tuple(index_at)].set(high)


def level_of(key, shape, shards, smallest, largest):
    def one(dim, parts):
        steps = jax.random.uniform(jax.random.fold_in(jax.random.fold_in(key, 6), dim), (parts,), jnp.float32, smallest / len(shards), largest / len(shards))
        return jnp.repeat(jnp.exp(steps), shape[dim] // parts).reshape((-1,) + (1,) * (len(shape) - dim - 1))

    gain = one(*shards[0])
    for cut in shards[1:]:
        gain = gain * one(*cut)
    return gain


def noise(rng, dims, deviation, most, cuts=(), kind=jnp.bfloat16):
    level = level_of(rng, dims, cuts, -0.22, 0.18) if cuts else 1.0
    drawn = jax.random.normal(rng, dims, jnp.float32) * deviation * level
    return jnp.minimum(jnp.maximum(drawn, -most), most).astype(kind)


def setup_inputs(seed: int = 0, part: int = 0) -> dict:
    key_of = jax.random.split(jax.random.key(seed), 8)
    own_keys = jax.random.split(jax.random.fold_in(key_of[7], part), 8)
    return {
        "strain": noise(key_of[0], (SLICES, DETS, TAPS + WIN), 1.0, 6.0, ((0, 4), (1, 2))),
        "filters": noise(own_keys[1], (SLICES, BASES, TAPS), TAPS ** -0.5, 0.125, ((0, 4),)),
        "recon_weights": noise(own_keys[2], (SLICES, ROWS, BASES), (BASES * N_CUTS) ** -0.5, 0.1875, ((0, 4),)),
        "row_spans": place_ends(jax.random.randint(own_keys[3], (ROWS,), 1, SLICES + 1), jax.random.fold_in(own_keys[3], 1), 1, SLICES).astype(jnp.int32),
        "slice_rates": draw_slice_rates(jax.random.fold_in(key_of[7], 71), part),
        "delays": place_ends(jax.random.randint(key_of[5], (DIRS, DETS), 0, MAXD), jax.random.fold_in(key_of[5], 1), 0, MAXD - 1).astype(jnp.int32),
        "antenna": jnp.clip(jax.random.uniform(key_of[6], (DIRS, DETS), jnp.float32, 0.2, 1.0), 0.2, 1.0),
    }


def filter_reference(samples, bank):
    size = 2 * TAPS + WIN
    spectrum = jnp.fft.rfft(samples.astype(jnp.float32), n=size)
    kernel = jnp.fft.rfft(bank.astype(jnp.float32), n=size, axis=1)
    convolved = jnp.fft.irfft(kernel * spectrum[None, :], n=size, axis=1)
    return convolved[:, TAPS:TAPS + WIN].astype(jnp.bfloat16)


def coherent(series, delays, antenna):
    detectors, height, window = series.shape
    padded = jnp.concatenate([series, jnp.zeros((detectors, height, MAXD), series.dtype)], axis=2)

    def direction(number, highest):
        summed = jnp.zeros((height, window), jnp.float32)
        for detector in range(detectors):
            shifted = lax.dynamic_slice_in_dim(padded[detector], delays[number, detector], window, 1)
            summed = summed + antenna[number, detector] * shifted
        return jnp.maximum(highest, jnp.abs(summed))

    return lax.fori_loop(0, delays.shape[0], direction, jnp.zeros((height, window), jnp.float32))


def reference(strain, filters, recon_weights, row_spans, slice_rates, delays, antenna):
    moments = jnp.arange(WIN, dtype=jnp.int32)

    def one_slice(total, inputs):
        samples, bank, weights, factor, number = inputs
        filtered = jax.vmap(filter_reference, in_axes=(0, None))(samples, bank)
        rebuilt = jnp.einsum("rb,kbw->krw", weights.astype(jnp.float32), filtered.astype(jnp.float32))
        keeping = (number < row_spans).astype(jnp.float32)
        terms = rebuilt * keeping[None, :, None]
        widened = jnp.take(terms, moments // factor, axis=2)
        return total + widened, None

    numbers = jnp.arange(SLICES, dtype=jnp.int32)
    combined, unused = lax.scan(one_slice, jnp.zeros((DETS, ROWS, WIN), jnp.float32), (strain, filters, recon_weights, slice_rates, numbers))
    return coherent(combined, delays, antenna)
```

```python
import functools

import jax
import jax.numpy as jnp
from jax import lax
from jax.experimental import pallas as pl
from jax.experimental.pallas import tpu as pltpu
from jax.sharding import PartitionSpec as P

MESH = pl.DeviceIdType.MESH
LANES = 128
WIDE = 256
BATCH = 2
LEVELS = 4
CHUNK = 64
GRANT = 16 * 2**20


def exchange_kernel(
    cuts, dets, spans_hbm, strain_hbm, weights_hbm, filters_hbm, rates_hbm, delays_hbm, antenna_hbm,
    bank_ref, series_ref, rates_ref, delays_ref, antenna_ref,
    spans_ref, strain_ref, weights_ref, filters, bank_stage, series_stage,
    bank_send, bank_recv, cross_send, cross_recv, side_send, side_recv,
    local_sem,
):
    me = lax.axis_index("cuts")
    core = lax.axis_index("det")
    barrier = pltpu.get_barrier_semaphore()
    for step in range(1, cuts):
        pl.semaphore_signal(
            barrier, inc=1, device_id={"cuts": lax.rem(me + step, cuts)}, device_id_type=MESH
        )
    for turn in range(1, dets):
        pl.semaphore_signal(
            barrier, inc=1, device_id={"det": lax.rem(core + turn, dets)}, device_id_type=MESH
        )

    fetches = [
        pltpu.make_async_copy(strain_hbm, strain_ref, local_sem.at[3]),
        pltpu.make_async_copy(spans_hbm, spans_ref, local_sem.at[4]),
        pltpu.make_async_copy(weights_hbm, weights_ref, local_sem.at[5]),
        pltpu.make_async_copy(filters_hbm, filters, local_sem.at[0]),
    ]
    for copy in fetches:
        copy.start()
    passed = [
        pltpu.make_async_copy(rates_hbm, rates_ref, local_sem.at[6]),
        pltpu.make_async_copy(delays_hbm, delays_ref, local_sem.at[7]),
        pltpu.make_async_copy(antenna_hbm, antenna_ref, local_sem.at[8]),
    ]
    for copy in passed:
        copy.start()
    fetches[0].wait()
    series_stage[...] = strain_ref[...].astype(jnp.float32)
    pl.semaphore_wait(barrier, cuts - 1 + dets - 1)
    mine = me * dets + core
    cross = []
    for step in range(1, cuts):
        cross.append(pltpu.make_async_remote_copy(
            src_ref=series_stage, dst_ref=series_ref.at[mine],
            send_sem=cross_send.at[step - 1], recv_sem=cross_recv.at[step - 1],
            device_id={"cuts": lax.rem(me + step, cuts)}, device_id_type=MESH,
        ))
    for copy in cross:
        copy.start()
    side = []
    for step in range(cuts):
        origin = lax.rem(me - step + cuts, cuts) * dets + core
        for turn in range(1, dets):
            number = step * (dets - 1) + turn - 1
            side.append(pltpu.make_async_remote_copy(
                src_ref=series_ref.at[origin] if step else series_stage, dst_ref=series_ref.at[origin],
                send_sem=side_send.at[number], recv_sem=side_recv.at[number],
                device_id={"det": lax.rem(core + turn, dets)}, device_id_type=MESH,
            ))
    for copy in side[: dets - 1]:
        copy.start()
    own = [
        pltpu.make_async_copy(series_stage, series_ref.at[mine], local_sem.at[1]),
        pltpu.make_async_copy(bank_stage.at[me], bank_ref.at[me], local_sem.at[2]),
    ]
    own[0].start()

    fetches[1].wait()
    fetches[2].wait()
    rows = weights_ref.shape[0]
    share = rows // cuts // dets
    live = (me < spans_ref[...]).astype(jnp.float32)
    across = lax.broadcasted_iota(jnp.int32, (rows, rows), 1)
    down = lax.broadcasted_iota(jnp.int32, (rows, rows), 0)
    keep = jnp.sum(jnp.where(across == down, live, 0.0), axis=1, keepdims=True)
    kept = (weights_ref[...].astype(jnp.float32) * keep).astype(jnp.bfloat16)
    parts = []
    for cut in range(cuts):
        low = kept[(cut * dets) * share : (cut * dets + 1) * share]
        for det in range(1, dets):
            other = kept[(cut * dets + det) * share : (cut * dets + det + 1) * share]
            low = jnp.where(core == det, other, low)
        parts.append(low)
    stacked = jnp.concatenate(parts, axis=0)
    fetches[3].wait()
    taps = filters.shape[1]
    for first in range(0, taps, WIDE):
        block = jnp.dot(stacked, filters[:, first : first + WIDE], preferred_element_type=jnp.float32)
        for cut in range(cuts):
            bank_stage[cut, :, first : first + WIDE] = block[cut * share : (cut + 1) * share]
    banks = []
    for step in range(1, cuts):
        target = lax.rem(me + step, cuts)
        banks.append(pltpu.make_async_remote_copy(
            src_ref=bank_stage.at[target], dst_ref=bank_ref.at[me],
            send_sem=bank_send.at[step - 1], recv_sem=bank_recv.at[step - 1],
            device_id={"cuts": target}, device_id_type=MESH,
        ))
    for copy in banks:
        copy.start()
    own[1].start()
    for step in range(1, cuts):
        cross[step - 1].wait_recv()
        for turn in range(1, dets):
            side[step * (dets - 1) + turn - 1].start()
    for copy in own + passed:
        copy.wait()
    for copy in cross:
        copy.wait_send()
    for copy in side:
        copy.wait()
    for copy in banks:
        copy.wait()


def exchange(spans, strain, filters, weights, rates, delays, antenna, cuts, dets):
    rows = weights.shape[0] // cuts // dets
    taps = filters.shape[1]
    length = strain.shape[-1]
    hbm = pl.BlockSpec(memory_space=pltpu.HBM)
    free = pl.BlockSpec(memory_space=pl.ANY)
    dma = pltpu.SemaphoreType.DMA
    return pl.pallas_call(
        functools.partial(exchange_kernel, cuts, dets),
        out_shape=(
            jax.ShapeDtypeStruct((cuts, rows, taps), jnp.float32),
            jax.ShapeDtypeStruct((cuts * dets, 1, length), jnp.float32),
            jax.ShapeDtypeStruct(rates.shape, rates.dtype),
            jax.ShapeDtypeStruct(delays.shape, delays.dtype),
            jax.ShapeDtypeStruct(antenna.shape, antenna.dtype),
        ),
        in_specs=[hbm] * 7,
        out_specs=(free,) * 5,
        scratch_shapes=[
            pltpu.VMEM(spans.shape, spans.dtype),
            pltpu.VMEM(strain.shape, strain.dtype),
            pltpu.VMEM(weights.shape, weights.dtype),
            pltpu.VMEM(filters.shape, filters.dtype),
            pltpu.VMEM((cuts, rows, taps), jnp.float32),
            pltpu.VMEM((1, length), jnp.float32),
            dma((cuts - 1,)),
            dma((cuts - 1,)),
            dma((cuts - 1,)),
            dma((cuts - 1,)),
            dma((cuts * (dets - 1),)),
            dma((cuts * (dets - 1),)),
            dma((9,)),
        ],
        compiler_params=pltpu.CompilerParams(collective_id=0, has_side_effects=True, vmem_limit_bytes=GRANT),
    )(*[pltpu.with_memory_space_constraint(x, pltpu.HBM) for x in (spans, strain, weights, filters, rates, delays, antenna)])


def search_kernel(
    rates_ref, delays_ref, antenna_ref, bank_ref, series_ref, peak_ref,
    even, odd, last, total, combined, turned, best,
):
    slices, rows, taps = bank_ref.shape
    dets = series_ref.shape[0] // slices
    window = peak_ref.shape[1]
    tiles = window // LANES
    pieces = taps // WIDE
    chunks = series_ref.shape[2] // LANES
    combined[...] = jnp.zeros(combined.shape, jnp.float32)
    lane = lax.broadcasted_iota(jnp.int32, (rows, LANES), 1)
    ahead = lax.broadcasted_iota(jnp.int32, (LANES, LANES), 1) >= lax.broadcasted_iota(
        jnp.int32, (LANES, LANES), 0
    )

    def build(keep, number, first, previous=None):
        for det in range(dets):
            if previous is not None:
                keep[det, 0] = previous[det, 2 * BATCH]
                before = last[det].astype(jnp.float32)
            for near in range(1, 2 * BATCH + 1):
                at = pl.multiple_of(jnp.clip(first + near + 1, 0, chunks - 1) * LANES, LANES)
                piece = series_ref[number * dets + det, :, pl.ds(at, LANES)]
                now = pltpu.roll(jnp.broadcast_to(piece, (LANES, LANES)), 0, 1, stride=1, stride_axis=0)
                if previous is not None or near > 1:
                    keep[det, near] = jnp.where(ahead, now, before).astype(jnp.bfloat16)
                before = now
            last[det] = before.astype(jnp.bfloat16)

    for det in range(dets):
        for near in range(2):
            even[det, near] = jnp.zeros((LANES, LANES), jnp.bfloat16)
    build(even, 0, -2)

    def one_slice(number, carry):
        rate = rates_ref[number]
        level = (rate > 1).astype(jnp.int32) + (rate > 3).astype(jnp.int32) + (rate > 7).astype(jnp.int32)
        blocks = lax.shift_right_logical(jnp.int32(window // WIDE), level)
        batches = (blocks + pieces + 2 * BATCH - 1) // (2 * BATCH)
        taps_all = bank_ref[number].astype(jnp.bfloat16)
        stacked = jnp.concatenate(
            [taps_all[:, piece * WIDE : (piece + 1) * WIDE] for piece in range(pieces)], axis=0
        )
        for det in range(dets):
            for at in range(2 * pieces - 2):
                total[det, at] = jnp.zeros((rows, LANES), jnp.float32)

        def multiply(keep, det, sums, start):
            for near in range(BATCH):
                low, middle, high = keep[det, 2 * near], keep[det, 2 * near + 1], keep[det, 2 * near + 2]
                square = jnp.concatenate(
                    [jnp.concatenate([middle, high], axis=1), jnp.concatenate([low, middle], axis=1)], axis=0
                )
                result = jnp.dot(stacked, square, preferred_element_type=jnp.float32)
                for piece in range(pieces):
                    term = result[piece * rows : (piece + 1) * rows]
                    old = sums[start + near + piece]
                    sums[start + near + piece] = term if old is None else old + term

        def convolve(batch, c):
            base = 2 * BATCH * batch
            sums = [[None] * (2 * BATCH + pieces - 1) for det in range(dets)]
            build(odd, number, 2 * base + 2 * BATCH - 2, even)
            for det in range(dets):
                multiply(even, det, sums[det], 0)
            final = batch == batches - 1
            build(
                even,
                jnp.where(final, jnp.minimum(number + 1, slices - 1), number),
                jnp.where(final, -2, 2 * base + 4 * BATCH - 2),
                odd,
            )
            for det in range(dets):
                multiply(odd, det, sums[det], BATCH)
                for far, value in enumerate(sums[det]):
                    for half in range(2):
                        at = 2 * (base + far) + half
                        part = value[:, half * LANES : (half + 1) * LANES]
                        total[det, at] = part if far >= pieces - 1 else total[det, at] + part
            return c

        lax.fori_loop(0, batches, convolve, 0)

        skip = 2 * pieces
        for known in range(LEVELS):
            @pl.when(level == known)
            def _(known=known):
                for tile in range(tiles):
                    index = lax.shift_right_logical(lane, known) + (tile % 2**known) * (LANES >> known)
                    for det in range(dets):
                        values = total[det, skip + (tile >> known)]
                        if known:
                            values = jnp.take_along_axis(values, index, axis=1)
                        combined[det, tile] += values
        return carry

    lax.fori_loop(0, slices, one_slice, 0)

    groups = LANES // rows
    apart = tiles // groups
    for det in range(dets):
        for offset in range(apart + 1):
            block = jnp.concatenate(
                [combined[det, group * apart + offset] for group in range(groups)], axis=0
            )
            turned[det, offset * LANES : (offset + 1) * LANES] = block.T

    for first in range(0, apart * LANES, CHUNK):
        def direction(number, highest):
            summed = None
            for det in range(dets):
                start = delays_ref[det, number] + first
                term = antenna_ref[det, number] * turned[det, pl.ds(start, CHUNK), :]
                summed = term if summed is None else summed + term
            return jnp.maximum(highest, jnp.abs(summed))

        best[first : first + CHUNK] = lax.fori_loop(
            0, delays_ref.shape[1], direction, jnp.zeros((CHUNK, LANES), jnp.float32), unroll=16
        )
    for offset in range(apart):
        back = best[offset * LANES : (offset + 1) * LANES].T
        for group in range(groups):
            at = (group * apart + offset) * LANES
            peak_ref[:, at : at + LANES] = back[group * rows : (group + 1) * rows]


def search(rates, delays, antenna, bank, series, window):
    slices, rows, taps = bank.shape
    dets = series.shape[0] // slices
    tiles = window // LANES
    pieces = taps // WIDE
    groups = LANES // rows
    apart = tiles // groups
    chunks = series.shape[2] // LANES
    smem = pl.BlockSpec(memory_space=pltpu.SMEM)
    vmem = pl.BlockSpec(memory_space=pltpu.VMEM)
    return pl.pallas_call(
        search_kernel,
        out_shape=jax.ShapeDtypeStruct((rows, window), jnp.float32),
        in_specs=[smem, smem, smem, vmem, vmem],
        out_specs=vmem,
        scratch_shapes=[
            pltpu.VMEM((dets, 2 * BATCH + 1, LANES, LANES), jnp.bfloat16),
            pltpu.VMEM((dets, 2 * BATCH + 1, LANES, LANES), jnp.bfloat16),
            pltpu.VMEM((dets, LANES, LANES), jnp.bfloat16),
            pltpu.VMEM((dets, chunks + 4 * BATCH + 2 * pieces, rows, LANES), jnp.float32),
            pltpu.VMEM((dets, tiles + apart, rows, LANES), jnp.float32),
            pltpu.VMEM((dets, (apart + 1) * LANES, LANES), jnp.float32),
            pltpu.VMEM((apart * LANES, LANES), jnp.float32),
        ],
        compiler_params=pltpu.CompilerParams(vmem_limit_bytes=GRANT),
    )(rates, delays, antenna, bank, series)


def shards(strain, filters, recon_weights, row_spans, slice_rates, delays, antenna):
    cuts = lax.axis_size("cuts")
    dets = lax.axis_size("det")
    bank, series, rates, delays, antenna = exchange(
        row_spans.reshape(1, -1), strain.reshape(1, -1), filters[0], recon_weights[0],
        slice_rates, delays.T, antenna.T, cuts, dets,
    )
    window = strain.shape[-1] - filters.shape[-1]
    return search(rates, delays, antenna, bank, series, window)


def solution(mesh):
    placed = (
        P("cuts", "det", None),
        P(("bank", "cuts"), None, None),
        P(("bank", "cuts"), None, None),
        P("bank"),
        P(),
        P(),
        P(),
    )
    return jax.shard_map(
        shards,
        mesh=mesh,
        in_specs=placed,
        out_specs=P(("bank", "cuts", "det"), None),
        check_vma=False,
    )
```

```python
import functools

import jax
import jax.numpy as jnp
from jax import lax
from jax.experimental import pallas as pl
from jax.experimental.pallas import tpu as pltpu
from jax.sharding import PartitionSpec as P

MESH = pl.DeviceIdType.MESH
LANES = 128
WIDE = 256
BATCH = 2
COARSEST = 8
CHUNK = 64
EARLY = 2
GRANT = 16 * 2**20


def partner(me, step):
    bit, other = 1, me
    while bit <= step:
        if step & bit:
            other = other + bit * (1 - 2 * lax.rem(lax.div(me, bit), 2))
        bit *= 2
    return other


def stack(bank, pieces):
    taps = bank.astype(jnp.bfloat16)
    return jnp.concatenate([taps[:, piece * WIDE : (piece + 1) * WIDE] for piece in range(pieces)], axis=0)


def convolve(stacked, fetch, dets, pieces, chunks, batches, even, odd, last, total):
    rows = stacked.shape[0] // pieces
    ahead = lax.broadcasted_iota(jnp.int32, (LANES, LANES), 1) >= lax.broadcasted_iota(
        jnp.int32, (LANES, LANES), 0
    )

    def build(keep, first, previous=None):
        for det in range(dets):
            if previous is not None:
                keep[det, 0] = previous[det, 2 * BATCH]
                before = last[det].astype(jnp.float32)
            for near in range(1, 2 * BATCH + 1):
                at = pl.multiple_of(jnp.minimum(first + near + 1, chunks - 1) * LANES, LANES)
                piece = fetch(det, at)
                now = pltpu.roll(jnp.broadcast_to(piece, (LANES, LANES)), 0, 1, stride=1, stride_axis=0)
                if previous is not None or near > 1:
                    keep[det, near] = jnp.where(ahead, now, before).astype(jnp.bfloat16)
                before = now
            last[det] = before.astype(jnp.bfloat16)

    def multiply(keep, det, sums, start):
        for near in range(BATCH):
            low, middle, high = keep[det, 2 * near], keep[det, 2 * near + 1], keep[det, 2 * near + 2]
            square = jnp.concatenate(
                [jnp.concatenate([middle, high], axis=1), jnp.concatenate([low, middle], axis=1)], axis=0
            )
            result = jnp.dot(stacked, square, preferred_element_type=jnp.float32)
            for piece in range(pieces):
                term = result[piece * rows : (piece + 1) * rows]
                old = sums[start + near + piece]
                sums[start + near + piece] = term if old is None else old + term

    for det in range(dets):
        for near in range(2):
            even[det, near] = jnp.zeros((LANES, LANES), jnp.bfloat16)
        for at in range(2 * pieces - 2):
            total[det, at] = jnp.zeros((rows, LANES), jnp.float32)
    build(even, -2)

    def one_batch(batch, carry):
        base = 2 * BATCH * batch
        sums = [[None] * (2 * BATCH + pieces - 1) for det in range(dets)]
        build(odd, 2 * base + 2 * BATCH - 2, even)
        for det in range(dets):
            multiply(even, det, sums[det], 0)
        build(even, 2 * base + 4 * BATCH - 2, odd)
        for det in range(dets):
            multiply(odd, det, sums[det], BATCH)
            for far, value in enumerate(sums[det]):
                for half in range(2):
                    at = 2 * (base + far) + half
                    part = value[:, half * LANES : (half + 1) * LANES]
                    total[det, at] = part if far >= pieces - 1 else total[det, at] + part
        return carry

    lax.fori_loop(0, batches, one_batch, 0)


def batches_of(blocks, pieces):
    return (blocks + pieces + 2 * BATCH - 1) // (2 * BATCH)


def exchange_kernel(
    cuts, dets, early,
    spans_hbm, strain_hbm, weights_hbm, filters_hbm, rates_hbm, delays_hbm, antenna_hbm,
    bank_ref, series_ref, partial_ref, rates_ref, delays_ref, antenna_ref,
    spans_ref, strain_ref, weights_ref, filters, bank_stage, bank_early, series, even, odd, last,
    bank_send, bank_recv, cross_send, cross_recv, side_send, side_recv,
    local_sem,
):
    me = lax.axis_index("cuts")
    core = lax.axis_index("det")
    barrier = pltpu.get_barrier_semaphore()
    for step in range(1, cuts):
        pl.semaphore_signal(
            barrier, inc=1, device_id={"cuts": partner(me, step)}, device_id_type=MESH
        )
    for turn in range(1, dets):
        pl.semaphore_signal(
            barrier, inc=1, device_id={"det": lax.rem(core + turn, dets)}, device_id_type=MESH
        )

    fetches = [
        pltpu.make_async_copy(strain_hbm, strain_ref, local_sem.at[0]),
        pltpu.make_async_copy(spans_hbm, spans_ref, local_sem.at[1]),
        pltpu.make_async_copy(weights_hbm, weights_ref, local_sem.at[2]),
        pltpu.make_async_copy(filters_hbm, filters, local_sem.at[3]),
        pltpu.make_async_copy(rates_hbm, rates_ref, local_sem.at[4]),
        pltpu.make_async_copy(delays_hbm, delays_ref, local_sem.at[5]),
        pltpu.make_async_copy(antenna_hbm, antenna_ref, local_sem.at[6]),
    ]
    for copy in fetches:
        copy.start()

    def series_at(step, det):
        if step <= early:
            return series.at[step * dets + det]
        return series_ref.at[(step - early - 1) * dets + det]

    def bank_at(step):
        return bank_early.at[step - 1] if step <= early else bank_ref.at[step - early - 1]

    fetches[0].wait()
    series[core] = strain_ref[...].astype(jnp.float32)
    pl.semaphore_wait(barrier, cuts - 1 + dets - 1)
    cross = []
    for step in range(1, cuts):
        cross.append(pltpu.make_async_remote_copy(
            src_ref=series_at(0, core), dst_ref=series_at(step, core),
            send_sem=cross_send.at[step - 1], recv_sem=cross_recv.at[step - 1],
            device_id={"cuts": partner(me, step)}, device_id_type=MESH,
        ))
    side = []
    for step in range(cuts):
        for turn in range(1, dets):
            number = step * (dets - 1) + turn - 1
            side.append(pltpu.make_async_remote_copy(
                src_ref=series_at(step, core), dst_ref=series_at(step, core),
                send_sem=side_send.at[number], recv_sem=side_recv.at[number],
                device_id={"det": lax.rem(core + turn, dets)}, device_id_type=MESH,
            ))
    for copy in cross:
        copy.start()
    for copy in side[: dets - 1]:
        copy.start()

    fetches[1].wait()
    fetches[2].wait()
    rows = weights_ref.shape[0]
    share = rows // cuts // dets
    live = (me < spans_ref[...]).astype(jnp.float32)
    across = lax.broadcasted_iota(jnp.int32, (rows, rows), 1)
    down = lax.broadcasted_iota(jnp.int32, (rows, rows), 0)
    keep = jnp.sum(jnp.where(across == down, live, 0.0), axis=1, keepdims=True)
    kept = (weights_ref[...].astype(jnp.float32) * keep).astype(jnp.bfloat16)
    parts = []
    for cut in range(cuts):
        low = kept[(cut * dets) * share : (cut * dets + 1) * share]
        for det in range(1, dets):
            other = kept[(cut * dets + det) * share : (cut * dets + det + 1) * share]
            low = jnp.where(core == det, other, low)
        parts.append(low)
    stacked = jnp.concatenate(parts, axis=0)
    fetches[3].wait()
    taps = filters.shape[1]
    for first in range(0, taps, WIDE):
        block = jnp.dot(stacked, filters[:, first : first + WIDE], preferred_element_type=jnp.float32)
        for cut in range(cuts):
            bank_stage[cut, :, first : first + WIDE] = block[cut * share : (cut + 1) * share]
    banks = []
    for step in range(1, cuts):
        target = partner(me, step)
        banks.append(pltpu.make_async_remote_copy(
            src_ref=bank_stage.at[target], dst_ref=bank_at(step),
            send_sem=bank_send.at[step - 1], recv_sem=bank_recv.at[step - 1],
            device_id={"cuts": target}, device_id_type=MESH,
        ))
    for copy in banks:
        copy.start()

    pieces = taps // WIDE
    length = series.shape[2]
    window = length - taps

    def filtered(step, bank):
        blocks = jnp.where(partner(me, step) == cuts - 1, window // COARSEST // WIDE, window // WIDE)
        convolve(
            stack(bank, pieces), lambda det, at: series[step * dets + det, :, pl.ds(at, LANES)],
            dets, pieces, length // LANES, lax.div(blocks + pieces + 2 * BATCH - 1, 2 * BATCH),
            even, odd, last, partial_ref.at[step],
        )

    for copy in side[: dets - 1]:
        copy.wait_recv()
    filtered(0, bank_stage[me])
    for step in range(1, cuts):
        cross[step - 1].wait_recv()
        for copy in side[step * (dets - 1) : (step + 1) * (dets - 1)]:
            copy.start()
    for step in range(1, early + 1):
        for copy in side[step * (dets - 1) : (step + 1) * (dets - 1)]:
            copy.wait_recv()
        banks[step - 1].wait_recv()
        filtered(step, bank_early[step - 1])
    for copy in fetches[4:]:
        copy.wait()
    for copy in side[(early + 1) * (dets - 1) :]:
        copy.wait_recv()
    for copy in banks[early:]:
        copy.wait_recv()
    for copy in cross + side + banks:
        copy.wait_send()


def total_tiles(length, taps):
    return length // LANES + 4 * BATCH + 2 * (taps // WIDE)


def exchange(spans, strain, filters, weights, rates, delays, antenna, cuts, dets, early):
    rows = weights.shape[0] // cuts // dets
    taps = filters.shape[1]
    length = strain.shape[-1]
    late = cuts - 1 - early
    hbm = pl.BlockSpec(memory_space=pltpu.HBM)
    free = pl.BlockSpec(memory_space=pl.ANY)
    vmem = pl.BlockSpec(memory_space=pltpu.VMEM)
    dma = pltpu.SemaphoreType.DMA
    square = (dets, 2 * BATCH + 1, LANES, LANES)
    return pl.pallas_call(
        functools.partial(exchange_kernel, cuts, dets, early),
        out_shape=(
            jax.ShapeDtypeStruct((late, rows, taps), jnp.float32),
            jax.ShapeDtypeStruct((late * dets, 1, length), jnp.float32),
            jax.ShapeDtypeStruct((1 + early, dets, total_tiles(length, taps), rows, LANES), jnp.float32),
            jax.ShapeDtypeStruct(rates.shape, rates.dtype),
            jax.ShapeDtypeStruct(delays.shape, delays.dtype),
            jax.ShapeDtypeStruct(antenna.shape, antenna.dtype),
        ),
        in_specs=[hbm] * 7,
        out_specs=(free, free, vmem, free, free, free),
        scratch_shapes=[
            pltpu.VMEM(spans.shape, spans.dtype),
            pltpu.VMEM(strain.shape, strain.dtype),
            pltpu.VMEM(weights.shape, weights.dtype),
            pltpu.VMEM(filters.shape, filters.dtype),
            pltpu.VMEM((cuts, rows, taps), jnp.float32),
            pltpu.VMEM((early, rows, taps), jnp.float32),
            pltpu.VMEM(((1 + early) * dets, 1, length), jnp.float32),
            pltpu.VMEM(square, jnp.bfloat16),
            pltpu.VMEM(square, jnp.bfloat16),
            pltpu.VMEM((dets, LANES, LANES), jnp.bfloat16),
            dma((cuts - 1,)),
            dma((cuts - 1,)),
            dma((cuts - 1,)),
            dma((cuts - 1,)),
            dma((cuts * (dets - 1),)),
            dma((cuts * (dets - 1),)),
            dma((7,)),
        ],
        compiler_params=pltpu.CompilerParams(collective_id=0, has_side_effects=True, vmem_limit_bytes=GRANT),
    )(*[pltpu.with_memory_space_constraint(x, pltpu.HBM)
        for x in (spans, strain, weights, filters, rates, delays, antenna)])


def search_kernel(
    early, rates_ref, delays_ref, antenna_ref, bank_ref, series_ref, partial_ref, peak_ref,
    even, odd, last, total, combined, turned, best,
):
    late, rows, taps = bank_ref.shape
    dets = series_ref.shape[0] // late
    window = peak_ref.shape[1]
    tiles = window // LANES
    pieces = taps // WIDE
    chunks = series_ref.shape[2] // LANES
    skip = 2 * pieces
    me = lax.axis_index("cuts")
    lane = lax.broadcasted_iota(jnp.int32, (rows, LANES), 1)

    def level_of(step):
        rate = rates_ref[me ^ step]
        return sum((rate >= 2**known).astype(jnp.int32) for known in range(1, COARSEST.bit_length()))

    def filtered(index):
        level = level_of(index + early + 1)
        blocks = lax.shift_right_logical(jnp.int32(window // WIDE), level)
        convolve(
            stack(bank_ref[index], pieces), lambda det, at: series_ref[index * dets + det, :, pl.ds(at, LANES)],
            dets, pieces, chunks, batches_of(blocks, pieces), even, odd, last, total,
        )
        return level

    def widen(level):
        narrow = lax.shift_right_logical(lane, level)
        width = lax.shift_right_logical(jnp.int32(LANES), level)
        rate = lax.shift_left(jnp.int32(1), level)

        def at(values, det, tile):
            index = narrow + (tile & (rate - 1)) * width
            source = values[det, skip + lax.shift_right_logical(jnp.int32(tile), level)]
            return jnp.take_along_axis(source, index, axis=1)

        return at

    if late > 1:
        for det in range(dets):
            for tile in range(tiles):
                combined[det, tile] = jnp.zeros((rows, LANES), jnp.float32)

        def one_slice(index, carry):
            at = widen(filtered(index))
            for tile in range(tiles):
                for det in range(dets):
                    combined[det, tile] += at(total, det, tile)
            return carry

        lax.fori_loop(0, late - 1, one_slice, 0)

    final = widen(filtered(late - 1))
    firsts = [widen(level_of(step)) for step in range(early + 1)]
    for tile in range(tiles):
        for det in range(dets):
            values = final(total, det, tile)
            for step, at in enumerate(firsts):
                values += at(partial_ref.at[step], det, tile)
            if late > 1:
                values += combined[det, tile]
            combined[det, tile] = values
    for det in range(dets):
        combined[det, tiles] = jnp.zeros((rows, LANES), jnp.float32)

    groups = LANES // rows
    apart = tiles // groups
    for det in range(dets):
        for offset in range(apart + 1):
            block = jnp.concatenate(
                [combined[det, group * apart + offset] for group in range(groups)], axis=0
            )
            turned[det, offset * LANES : (offset + 1) * LANES] = block.T

    for first in range(0, apart * LANES, CHUNK):
        def direction(number, highest):
            summed = None
            for det in range(dets):
                start = delays_ref[det, number] + first
                term = antenna_ref[det, number] * turned[det, pl.ds(start, CHUNK), :]
                summed = term if summed is None else summed + term
            return jnp.maximum(highest, jnp.abs(summed))

        best[first : first + CHUNK] = lax.fori_loop(
            0, delays_ref.shape[1], direction, jnp.zeros((CHUNK, LANES), jnp.float32), unroll=16
        )
    for offset in range(apart):
        back = best[offset * LANES : (offset + 1) * LANES].T
        for group in range(groups):
            at = (group * apart + offset) * LANES
            peak_ref[:, at : at + LANES] = back[group * rows : (group + 1) * rows]


def search(rates, delays, antenna, bank, series, partial, window, early):
    late, rows, taps = bank.shape
    dets = series.shape[0] // late
    tiles = window // LANES
    groups = LANES // rows
    apart = tiles // groups
    smem = pl.BlockSpec(memory_space=pltpu.SMEM)
    vmem = pl.BlockSpec(memory_space=pltpu.VMEM)
    square = (dets, 2 * BATCH + 1, LANES, LANES)
    return pl.pallas_call(
        functools.partial(search_kernel, early),
        out_shape=jax.ShapeDtypeStruct((rows, window), jnp.float32),
        in_specs=[smem, smem, smem, vmem, vmem, vmem],
        out_specs=vmem,
        scratch_shapes=[
            pltpu.VMEM(square, jnp.bfloat16),
            pltpu.VMEM(square, jnp.bfloat16),
            pltpu.VMEM((dets, LANES, LANES), jnp.bfloat16),
            pltpu.VMEM((dets, total_tiles(window + taps, taps), rows, LANES), jnp.float32),
            pltpu.VMEM((dets, tiles + 1, rows, LANES), jnp.float32),
            pltpu.VMEM((dets, (apart + 1) * LANES, LANES), jnp.float32),
            pltpu.VMEM((apart * LANES, LANES), jnp.float32),
        ],
        compiler_params=pltpu.CompilerParams(vmem_limit_bytes=GRANT),
    )(rates, delays, antenna, bank, series, partial)


def shards(strain, filters, recon_weights, row_spans, slice_rates, delays, antenna):
    cuts = lax.axis_size("cuts")
    dets = lax.axis_size("det")
    early = min(EARLY, cuts - 2)
    bank, series, partial, rates, delays, antenna = exchange(
        row_spans.reshape(1, -1), strain.reshape(1, -1), filters[0], recon_weights[0],
        slice_rates, delays.T, antenna.T, cuts, dets, early,
    )
    window = strain.shape[-1] - filters.shape[-1]
    return search(rates, delays, antenna, bank, series, partial, window, early)


def solution(mesh):
    placed = (
        P("cuts", "det", None),
        P(("bank", "cuts"), None, None),
        P(("bank", "cuts"), None, None),
        P("bank"),
        P(),
        P(),
        P(),
    )
    return jax.shard_map(
        shards,
        mesh=mesh,
        in_specs=placed,
        out_specs=P(("bank", "cuts", "det"), None),
        check_vma=False,
    )
```

```python
import functools

import jax
import jax.numpy as jnp
from jax import lax
from jax.experimental import pallas as pl
from jax.experimental.pallas import tpu as pltpu
from jax.sharding import PartitionSpec as P

MESH = pl.DeviceIdType.MESH
LANES = 128
WIDE = 256
BATCH = 4
DEEP = 16
COARSEST = 8
HALO = 48
CHUNK = 64
EARLY = 1
READY = 2
GRANT = 24 * 2**20


def partner(me, step):
    bit, other = 1, me
    while bit <= step:
        if step & bit:
            other = other + bit * (1 - 2 * lax.rem(lax.div(me, bit), 2))
        bit *= 2
    return other


def batches_of(blocks, pieces):
    return (blocks + pieces - 1 + BATCH - 1) // BATCH


def total_tiles(length, taps):
    pieces = taps // WIDE
    return 2 * (BATCH * batches_of((length - taps) // WIDE, pieces) + pieces - 1)


def tile_count(length, taps):
    return 2 * BATCH * batches_of((length - taps) // WIDE, taps // WIDE) + 2


def fill(fetch, tiles, dets, chunks):
    deep = next(deep for deep in range(DEEP, 0, -1) if chunks % deep == 0)
    ahead = lax.broadcasted_iota(jnp.int32, (LANES, LANES), 1) >= lax.broadcasted_iota(
        jnp.int32, (LANES, LANES), 0
    )

    def some(number, carry):
        left = []
        for det, before in zip(dets, carry):
            for near in range(deep):
                chunk = number * deep + near
                piece = fetch(det, pl.multiple_of(chunk * LANES, LANES))
                now = pltpu.roll(jnp.broadcast_to(piece, (LANES, LANES)), 0, 1, stride=1, stride_axis=0)
                tiles[det, chunk] = jnp.where(ahead, now, before).astype(jnp.bfloat16)
                before = now
            left.append(before)
        return tuple(left)

    lax.fori_loop(0, chunks // deep, some, tuple(jnp.zeros((LANES, LANES), jnp.float32) for det in dets))


def stack(bank, pieces):
    taps = bank.astype(jnp.bfloat16)
    return jnp.concatenate([taps[:, piece * WIDE : (piece + 1) * WIDE] for piece in range(pieces)], axis=0)


def convolve(stacked, tiles, dets, pieces, batches, total):
    rows = stacked.shape[0] // pieces

    def one_batch(batch, carry):
        base = BATCH * batch
        for det in dets:
            sums = [None] * (BATCH + pieces - 1)
            for near in range(BATCH):
                first = 2 * (base + near) + 1
                low, middle, high = tiles[det, first], tiles[det, first + 1], tiles[det, first + 2]
                square = jnp.concatenate(
                    [jnp.concatenate([middle, high], axis=1), jnp.concatenate([low, middle], axis=1)], axis=0
                )
                result = jnp.dot(stacked, square, preferred_element_type=jnp.float32)
                for piece in range(pieces):
                    term = result[piece * rows : (piece + 1) * rows]
                    old = sums[near + piece]
                    sums[near + piece] = term if old is None else old + term
            for far, value in enumerate(sums):
                for half in range(2):
                    at = 2 * (base + far) + half
                    part = value[:, half * LANES : (half + 1) * LANES]
                    total[det, at] = part if far >= pieces - 1 else total[det, at] + part
        return carry

    lax.fori_loop(0, batches, one_batch, 0)


def exchange_kernel(
    cuts, dets, early, ready,
    spans_hbm, strain_hbm, weights_hbm, filters_hbm, rates_hbm, delays_hbm, antenna_hbm,
    bank_ref, series_ref, partial_ref, tiles_ref, rates_ref, delays_ref, antenna_ref,
    spans_ref, strain_ref, weights_ref, filters, bank_stage, bank_early, series, tiles,
    bank_send, bank_recv, cross_send, cross_recv, side_send, side_recv,
    local_sem,
):
    me = lax.axis_index("cuts")
    core = lax.axis_index("det")
    barrier = pltpu.get_barrier_semaphore()
    for step in range(1, cuts):
        pl.semaphore_signal(
            barrier, inc=1, device_id={"cuts": partner(me, step)}, device_id_type=MESH
        )
    for turn in range(1, dets):
        pl.semaphore_signal(
            barrier, inc=1, device_id={"det": lax.rem(core + turn, dets)}, device_id_type=MESH
        )

    fetches = [
        pltpu.make_async_copy(strain_hbm, strain_ref, local_sem.at[0]),
        pltpu.make_async_copy(spans_hbm, spans_ref, local_sem.at[1]),
        pltpu.make_async_copy(weights_hbm, weights_ref, local_sem.at[2]),
        pltpu.make_async_copy(filters_hbm, filters, local_sem.at[3]),
        pltpu.make_async_copy(rates_hbm, rates_ref, local_sem.at[4]),
        pltpu.make_async_copy(delays_hbm, delays_ref, local_sem.at[5]),
        pltpu.make_async_copy(antenna_hbm, antenna_ref, local_sem.at[6]),
    ]
    for copy in fetches:
        copy.start()
    held = early + ready

    def series_at(step, det):
        if step <= held:
            return series.at[step * dets + det]
        return series_ref.at[(step - held - 1) * dets + det]

    def bank_at(step):
        return bank_early.at[step - 1] if step <= early else bank_ref.at[step - early - 1]

    fetches[0].wait()
    series[core] = strain_ref[...].astype(jnp.float32)
    pl.semaphore_wait(barrier, cuts - 1 + dets - 1)
    cross = []
    for step in range(1, cuts):
        cross.append(pltpu.make_async_remote_copy(
            src_ref=series_at(0, core), dst_ref=series_at(step, core),
            send_sem=cross_send.at[step - 1], recv_sem=cross_recv.at[step - 1],
            device_id={"cuts": partner(me, step)}, device_id_type=MESH,
        ))
    side = []
    for step in range(cuts):
        for turn in range(1, dets):
            number = step * (dets - 1) + turn - 1
            side.append(pltpu.make_async_remote_copy(
                src_ref=series_at(step, core), dst_ref=series_at(step, core),
                send_sem=side_send.at[number], recv_sem=side_recv.at[number],
                device_id={"det": lax.rem(core + turn, dets)}, device_id_type=MESH,
            ))
    for copy in cross:
        copy.start()
    for copy in side[: dets - 1]:
        copy.start()

    fetches[1].wait()
    fetches[2].wait()
    rows = weights_ref.shape[0]
    share = rows // cuts // dets
    live = (me < spans_ref[...]).astype(jnp.float32)
    across = lax.broadcasted_iota(jnp.int32, (rows, rows), 1)
    down = lax.broadcasted_iota(jnp.int32, (rows, rows), 0)
    keep = jnp.sum(jnp.where(across == down, live, 0.0), axis=1, keepdims=True)
    kept = (weights_ref[...].astype(jnp.float32) * keep).astype(jnp.bfloat16)
    parts = []
    for cut in range(cuts):
        low = kept[(cut * dets) * share : (cut * dets + 1) * share]
        for det in range(1, dets):
            other = kept[(cut * dets + det) * share : (cut * dets + det + 1) * share]
            low = jnp.where(core == det, other, low)
        parts.append(low)
    stacked = jnp.concatenate(parts, axis=0)
    fetches[3].wait()
    taps = filters.shape[1]
    for first in range(0, taps, WIDE):
        block = jnp.dot(stacked, filters[:, first : first + WIDE], preferred_element_type=jnp.float32)
        for cut in range(cuts):
            bank_stage[cut, :, first : first + WIDE] = block[cut * share : (cut + 1) * share]
    banks = []
    for step in range(1, cuts):
        target = partner(me, step)
        banks.append(pltpu.make_async_remote_copy(
            src_ref=bank_stage.at[target], dst_ref=bank_at(step),
            send_sem=bank_send.at[step - 1], recv_sem=bank_recv.at[step - 1],
            device_id={"cuts": target}, device_id_type=MESH,
        ))
    for copy in banks:
        copy.start()

    pieces = taps // WIDE
    length = series.shape[2]
    window = length - taps
    chunks = length // LANES

    def prepare(step, which, out):
        fill(lambda det, at: series[step * dets + det, :, pl.ds(at, LANES)], out, which, chunks)

    def filtered(step, which, bank):
        full = batches_of(window // WIDE, pieces)
        short = batches_of(window // COARSEST // WIDE, pieces)
        batches = jnp.where(partner(me, step) == cuts - 1, short, full)
        convolve(stack(bank, pieces), tiles.at[step], which, pieces, batches, partial_ref.at[step])

    everyone = list(range(dets))
    prepare(0, [core], tiles.at[0])
    filtered(0, [core], bank_stage[me])
    for copy in side[: dets - 1]:
        copy.wait_recv()
    for turn in range(1, dets):
        other = lax.rem(core + turn, dets)
        prepare(0, [other], tiles.at[0])
        filtered(0, [other], bank_stage[me])
    for step in range(1, cuts):
        cross[step - 1].wait_recv()
        for copy in side[step * (dets - 1) : (step + 1) * (dets - 1)]:
            copy.start()
    for step in range(1, held + 1):
        for copy in side[step * (dets - 1) : (step + 1) * (dets - 1)]:
            copy.wait_recv()
        prepare(step, everyone, tiles.at[step] if step <= early else tiles_ref.at[step - early - 1])
    for step in range(1, early + 1):
        banks[step - 1].wait_recv()
        filtered(step, everyone, bank_early[step - 1])
    for copy in fetches[4:]:
        copy.wait()
    for copy in side[(held + 1) * (dets - 1) :]:
        copy.wait_recv()
    for copy in banks[early:]:
        copy.wait_recv()
    for copy in cross + side + banks:
        copy.wait_send()


def exchange(spans, strain, filters, weights, rates, delays, antenna, cuts, dets, early, ready):
    rows = weights.shape[0] // cuts // dets
    taps = filters.shape[1]
    length = strain.shape[-1]
    late = cuts - 1 - early
    rest = max(late - ready, 1)
    hbm = pl.BlockSpec(memory_space=pltpu.HBM)
    free = pl.BlockSpec(memory_space=pl.ANY)
    vmem = pl.BlockSpec(memory_space=pltpu.VMEM)
    dma = pltpu.SemaphoreType.DMA
    squares = (dets, tile_count(length, taps), LANES, LANES)
    return pl.pallas_call(
        functools.partial(exchange_kernel, cuts, dets, early, ready),
        out_shape=(
            jax.ShapeDtypeStruct((late, rows, taps), jnp.float32),
            jax.ShapeDtypeStruct((rest * dets, 1, length), jnp.float32),
            jax.ShapeDtypeStruct((1 + early, dets, total_tiles(length, taps), rows, LANES), jnp.float32),
            jax.ShapeDtypeStruct((ready, *squares), jnp.bfloat16),
            jax.ShapeDtypeStruct(rates.shape, rates.dtype),
            jax.ShapeDtypeStruct(delays.shape, delays.dtype),
            jax.ShapeDtypeStruct(antenna.shape, antenna.dtype),
        ),
        in_specs=[hbm] * 7,
        out_specs=(free, free, vmem, vmem, free, free, free),
        scratch_shapes=[
            pltpu.VMEM(spans.shape, spans.dtype),
            pltpu.VMEM(strain.shape, strain.dtype),
            pltpu.VMEM(weights.shape, weights.dtype),
            pltpu.VMEM(filters.shape, filters.dtype),
            pltpu.VMEM((cuts, rows, taps), jnp.float32),
            pltpu.VMEM((early, rows, taps), jnp.float32),
            pltpu.VMEM(((1 + early + ready) * dets, 1, length), jnp.float32),
            pltpu.VMEM((1 + early, *squares), jnp.bfloat16),
            dma((cuts - 1,)),
            dma((cuts - 1,)),
            dma((cuts - 1,)),
            dma((cuts - 1,)),
            dma((cuts * (dets - 1),)),
            dma((cuts * (dets - 1),)),
            dma((7,)),
        ],
        compiler_params=pltpu.CompilerParams(collective_id=0, has_side_effects=True, vmem_limit_bytes=GRANT),
    )(*[pltpu.with_memory_space_constraint(x, pltpu.HBM)
        for x in (spans, strain, weights, filters, rates, delays, antenna)])


def search_kernel(
    early, ready, rates_ref, delays_ref, antenna_ref, bank_ref, series_ref, partial_ref, tiles_ref, peak_ref,
    total, turned, best, *squares,
):
    late, rows, taps = bank_ref.shape
    dets = partial_ref.shape[1]
    window = peak_ref.shape[1]
    length = series_ref.shape[2]
    pieces = taps // WIDE
    skip = 2 * (pieces - 1)
    everyone = list(range(dets))
    me = lax.axis_index("cuts")

    groups = LANES // rows
    apart = window // LANES // groups
    span = apart * LANES
    split = max(1, COARSEST // apart)
    ways = groups // split
    group_at = [place % ways * split + place // ways for place in range(groups)]

    def level_of(step):
        rate = rates_ref[me ^ step]
        return sum((rate >= 2**known).astype(jnp.int32) for known in range(1, COARSEST.bit_length()))

    def filtered(index, tiles, level):
        blocks = lax.shift_right_logical(jnp.int32(window // WIDE), level)
        convolve(stack(bank_ref[index], pieces), tiles, everyone, pieces, batches_of(blocks, pieces), total)

    def widen(values, level):
        for known in range(COARSEST.bit_length()):
            @pl.when(level == known)
            def _(known=known):
                rate = 2**known
                per = apart // rate
                for det in range(dets):
                    blocks = []
                    for near in range(per):
                        block = jnp.concatenate(
                            [values[det, skip + group * per + near] for group in group_at], axis=0
                        )
                        blocks.append((near * LANES, block.T))
                    if not per:
                        block = jnp.concatenate([values[det, skip + way] for way in range(ways)], axis=0).T
                        part = LANES // split
                        blocks = [(0, jnp.concatenate(
                            [block[turn * part : (turn + 1) * part] for turn in range(split)], axis=1
                        ))]
                    for first, block in blocks:
                        size = block.shape[0]
                        for turn in range(rate):
                            if rate > 1:
                                place = pl.ds(first * rate + turn, size, stride=rate)
                            else:
                                place = pl.ds(first, size)
                            turned[det, place, :] += block

    for det in range(dets):
        turned[det] = jnp.zeros(turned.shape[1:], jnp.float32)
    for step in range(early + 1):
        widen(partial_ref.at[step], level_of(step))
    for index in range(ready):
        level = level_of(early + 1 + index)
        filtered(index, tiles_ref.at[index], level)
        widen(total, level)
    if late > ready:
        def one_slice(index, carry):
            level = level_of(early + 1 + index)
            fill(
                lambda det, at: series_ref[(index - ready) * dets + det, :, pl.ds(at, LANES)],
                squares[0], everyone, length // LANES,
            )
            filtered(index, squares[0], level)
            widen(total, level)
            return carry

        lax.fori_loop(ready, late, one_slice, 0)

    lane = lax.broadcasted_iota(jnp.int32, (HALO, LANES), 1)
    row, place = lane & (rows - 1), lane // rows
    group = (place & (ways - 1)) * split + place // ways
    later = jnp.minimum(group + 1, groups - 1)
    source = ((later & (split - 1)) * ways + later // split) * rows + row
    for det in range(dets):
        following = jnp.take_along_axis(turned[det, :HALO], source, axis=1)
        turned[det, span : span + HALO] = jnp.where(group == groups - 1, 0.0, following)

    for first in range(0, span, CHUNK):
        def direction(number, highest):
            summed = None
            for det in range(dets):
                start = delays_ref[det, number] + first
                term = antenna_ref[det, number] * turned[det, pl.ds(start, CHUNK), :]
                summed = term if summed is None else summed + term
            return jnp.maximum(highest, jnp.abs(summed))

        best[first : first + CHUNK] = lax.fori_loop(
            0, delays_ref.shape[1], direction, jnp.zeros((CHUNK, LANES), jnp.float32), unroll=16
        )
    for near in range(apart):
        back = best[near * LANES : (near + 1) * LANES].T
        for place, group in enumerate(group_at):
            at = (group * apart + near) * LANES
            peak_ref[:, at : at + LANES] = back[place * rows : (place + 1) * rows]


def search(rates, delays, antenna, bank, series, partial, tiles, window, early):
    late, rows, taps = bank.shape
    ready = tiles.shape[0]
    dets = partial.shape[1]
    span = window // (LANES // rows)
    smem = pl.BlockSpec(memory_space=pltpu.SMEM)
    vmem = pl.BlockSpec(memory_space=pltpu.VMEM)
    return pl.pallas_call(
        functools.partial(search_kernel, early, ready),
        out_shape=jax.ShapeDtypeStruct((rows, window), jnp.float32),
        in_specs=[smem, smem, smem, vmem, vmem, vmem, vmem],
        out_specs=vmem,
        scratch_shapes=[
            pltpu.VMEM(partial.shape[1:], jnp.float32),
            pltpu.VMEM((dets, span + HALO, LANES), jnp.float32),
            pltpu.VMEM((span, LANES), jnp.float32),
        ] + [pltpu.VMEM(tiles.shape[1:], tiles.dtype)] * (late > ready),
        compiler_params=pltpu.CompilerParams(vmem_limit_bytes=GRANT),
    )(rates, delays, antenna, bank, series, partial, tiles)


def shards(strain, filters, recon_weights, row_spans, slice_rates, delays, antenna):
    cuts = lax.axis_size("cuts")
    dets = lax.axis_size("det")
    early = min(EARLY, cuts - 2)
    ready = min(READY, cuts - 1 - early)
    bank, series, partial, tiles, rates, delays, antenna = exchange(
        row_spans.reshape(1, -1), strain.reshape(1, -1), filters[0], recon_weights[0],
        slice_rates, delays.T, antenna.T, cuts, dets, early, ready,
    )
    window = strain.shape[-1] - filters.shape[-1]
    return search(rates, delays, antenna, bank, series, partial, tiles, window, early)


def solution(mesh):
    placed = (
        P("cuts", "det", None),
        P(("bank", "cuts"), None, None),
        P(("bank", "cuts"), None, None),
        P("bank"),
        P(),
        P(),
        P(),
    )
    return jax.shard_map(
        shards,
        mesh=mesh,
        in_specs=placed,
        out_specs=P(("bank", "cuts", "det"), None),
        check_vma=False,
    )
```

```python
import functools

import jax
import jax.numpy as jnp
from jax import lax
from jax.experimental import pallas as pl
from jax.experimental.pallas import tpu as pltpu
from jax.sharding import PartitionSpec as P

MESH = pl.DeviceIdType.MESH
LANES = 128
WIDE = 256
BATCH = 4
DEEP = 48
COARSEST = 8
HALO = 48
CHUNK = 64
EARLY = 1
READY = 2
GRANT = 24 * 2**20


def partner(me, step):
    bit, other = 1, me
    while bit <= step:
        if step & bit:
            other = other + bit * (1 - 2 * lax.rem(lax.div(me, bit), 2))
        bit *= 2
    return other


def batches_of(blocks, pieces):
    return (blocks + pieces - 1 + BATCH - 1) // BATCH


def total_tiles(length, taps):
    pieces = taps // WIDE
    return 2 * (BATCH * batches_of((length - taps) // WIDE, pieces) + pieces - 1)


def tile_count(length, taps):
    return 2 * BATCH * batches_of((length - taps) // WIDE, taps // WIDE) + 2


def fill(fetch, tiles, dets, chunks):
    deep = next(deep for deep in range(DEEP, 0, -1) if chunks % deep == 0)
    ahead = lax.broadcasted_iota(jnp.int32, (LANES, LANES), 1) >= lax.broadcasted_iota(
        jnp.int32, (LANES, LANES), 0
    )

    def some(number, carry):
        left = []
        for det, before in zip(dets, carry):
            for near in range(deep):
                chunk = number * deep + near
                piece = fetch(det, pl.multiple_of(chunk * LANES, LANES))
                now = pltpu.roll(jnp.broadcast_to(piece, (LANES, LANES)), 0, 1, stride=1, stride_axis=0)
                tiles[det, chunk] = jnp.where(ahead, now, before).astype(jnp.bfloat16)
                before = now
            left.append(before)
        return tuple(left)

    lax.fori_loop(0, chunks // deep, some, tuple(jnp.zeros((LANES, LANES), jnp.float32) for det in dets))


def stack(bank, pieces):
    taps = bank.astype(jnp.bfloat16)
    return jnp.concatenate([taps[:, piece * WIDE : (piece + 1) * WIDE] for piece in range(pieces)], axis=0)


def convolve(stacked, tiles, dets, pieces, batches, total):
    rows = stacked.shape[0] // pieces

    def one_batch(batch, carry):
        base = BATCH * batch
        for det in dets:
            sums = [None] * (BATCH + pieces - 1)
            for near in range(BATCH):
                first = 2 * (base + near) + 1
                low, middle, high = tiles[det, first], tiles[det, first + 1], tiles[det, first + 2]
                square = jnp.concatenate(
                    [jnp.concatenate([middle, high], axis=1), jnp.concatenate([low, middle], axis=1)], axis=0
                )
                result = jnp.dot(stacked, square, preferred_element_type=jnp.float32)
                for piece in range(pieces):
                    term = result[piece * rows : (piece + 1) * rows]
                    old = sums[near + piece]
                    sums[near + piece] = term if old is None else old + term
            for far, value in enumerate(sums):
                for half in range(2):
                    at = 2 * (base + far) + half
                    part = value[:, half * LANES : (half + 1) * LANES]
                    total[det, at] = part if far >= pieces - 1 else total[det, at] + part
        return carry

    lax.fori_loop(0, batches, one_batch, 0)


def convolve_building(stacked, fetch, dets, pieces, chunks, batches, even, odd, last, total, between=None):
    rows = stacked.shape[0] // pieces
    half = BATCH // 2
    ahead = lax.broadcasted_iota(jnp.int32, (LANES, LANES), 1) >= lax.broadcasted_iota(
        jnp.int32, (LANES, LANES), 0
    )

    def shifted(det, chunk):
        piece = fetch(det, pl.multiple_of(chunk * LANES, LANES))
        return pltpu.roll(jnp.broadcast_to(piece, (LANES, LANES)), 0, 1, stride=1, stride_axis=0)

    def build(keep, first, previous):
        for det in dets:
            keep[det, 0] = previous[det, 2 * half]
            before = last[det].astype(jnp.float32)
            for near in range(1, 2 * half + 1):
                now = shifted(det, jnp.minimum(first + near, chunks - 1))
                keep[det, near] = jnp.where(ahead, now, before).astype(jnp.bfloat16)
                before = now
            last[det] = before.astype(jnp.bfloat16)

    def multiply(keep, det, sums, start):
        for near in range(half):
            low, middle, high = keep[det, 2 * near], keep[det, 2 * near + 1], keep[det, 2 * near + 2]
            square = jnp.concatenate(
                [jnp.concatenate([middle, high], axis=1), jnp.concatenate([low, middle], axis=1)], axis=0
            )
            result = jnp.dot(stacked, square, preferred_element_type=jnp.float32)
            for piece in range(pieces):
                term = result[piece * rows : (piece + 1) * rows]
                old = sums[start + near + piece]
                sums[start + near + piece] = term if old is None else old + term

    for det in dets:
        before = shifted(det, 0)
        for near in range(2 * half + 1):
            now = shifted(det, near + 1)
            even[det, near] = jnp.where(ahead, now, before).astype(jnp.bfloat16)
            before = now
        last[det] = before.astype(jnp.bfloat16)

    def one_batch(batch, carry):
        base = BATCH * batch
        sums = [[None] * (BATCH + pieces - 1) for det in dets]
        build(odd, 2 * base + 2 * half + 1, even)
        for det in dets:
            multiply(even, det, sums[det], 0)
        build(even, 2 * base + 4 * half + 1, odd)
        for det in dets:
            multiply(odd, det, sums[det], half)
            for far, value in enumerate(sums[det]):
                for side in range(2):
                    at = 2 * (base + far) + side
                    part = value[:, side * LANES : (side + 1) * LANES]
                    total[det, at] = part if far >= pieces - 1 else total[det, at] + part
        return carry

    if between is None:
        lax.fori_loop(0, batches, one_batch, 0)
    else:
        middle = lax.div(batches, 2)
        lax.fori_loop(0, middle, one_batch, 0)
        between()
        lax.fori_loop(middle, batches, one_batch, 0)


def exchange_kernel(
    cuts, dets, early, ready,
    spans_hbm, strain_hbm, weights_hbm, filters_hbm, rates_hbm, delays_hbm, antenna_hbm,
    bank_ref, series_ref, partial_ref, tiles_ref, rates_ref, delays_ref, antenna_ref,
    spans_ref, strain_ref, weights_ref, filters, bank_stage, bank_early, series, even, odd, last,
    bank_send, bank_recv, cross_send, cross_recv, side_send, side_recv,
    local_sem,
):
    me = lax.axis_index("cuts")
    core = lax.axis_index("det")
    barrier = pltpu.get_barrier_semaphore()
    for step in range(1, cuts):
        pl.semaphore_signal(
            barrier, inc=1, device_id={"cuts": partner(me, step)}, device_id_type=MESH
        )
    for turn in range(1, dets):
        pl.semaphore_signal(
            barrier, inc=1, device_id={"det": lax.rem(core + turn, dets)}, device_id_type=MESH
        )

    fetches = [
        pltpu.make_async_copy(strain_hbm, strain_ref, local_sem.at[0]),
        pltpu.make_async_copy(spans_hbm, spans_ref, local_sem.at[1]),
        pltpu.make_async_copy(weights_hbm, weights_ref, local_sem.at[2]),
        pltpu.make_async_copy(filters_hbm, filters, local_sem.at[3]),
        pltpu.make_async_copy(rates_hbm, rates_ref, local_sem.at[4]),
        pltpu.make_async_copy(delays_hbm, delays_ref, local_sem.at[5]),
        pltpu.make_async_copy(antenna_hbm, antenna_ref, local_sem.at[6]),
    ]
    for copy in fetches:
        copy.start()
    held = early + ready

    def series_at(step, det):
        if step <= held:
            return series.at[step * dets + det]
        return series_ref.at[(step - held - 1) * dets + det]

    def bank_at(step):
        return bank_early.at[step - 1] if step <= early else bank_ref.at[step - early - 1]

    fetches[0].wait()
    series[core] = strain_ref[...].astype(jnp.float32)
    pl.semaphore_wait(barrier, cuts - 1 + dets - 1)
    cross = []
    for step in range(1, cuts):
        cross.append(pltpu.make_async_remote_copy(
            src_ref=series_at(0, core), dst_ref=series_at(step, core),
            send_sem=cross_send.at[step - 1], recv_sem=cross_recv.at[step - 1],
            device_id={"cuts": partner(me, step)}, device_id_type=MESH,
        ))
    side = []
    for step in range(cuts):
        for turn in range(1, dets):
            number = step * (dets - 1) + turn - 1
            side.append(pltpu.make_async_remote_copy(
                src_ref=series_at(step, core), dst_ref=series_at(step, core),
                send_sem=side_send.at[number], recv_sem=side_recv.at[number],
                device_id={"det": lax.rem(core + turn, dets)}, device_id_type=MESH,
            ))
    for copy in cross:
        copy.start()
    for copy in side[: dets - 1]:
        copy.start()

    fetches[1].wait()
    fetches[2].wait()
    rows = weights_ref.shape[0]
    share = rows // cuts // dets
    live = (me < spans_ref[...]).astype(jnp.float32)
    across = lax.broadcasted_iota(jnp.int32, (rows, rows), 1)
    down = lax.broadcasted_iota(jnp.int32, (rows, rows), 0)
    keep = jnp.sum(jnp.where(across == down, live, 0.0), axis=1, keepdims=True)
    kept = (weights_ref[...].astype(jnp.float32) * keep).astype(jnp.bfloat16)
    parts = []
    for cut in range(cuts):
        low = kept[(cut * dets) * share : (cut * dets + 1) * share]
        for det in range(1, dets):
            other = kept[(cut * dets + det) * share : (cut * dets + det + 1) * share]
            low = jnp.where(core == det, other, low)
        parts.append(low)
    stacked = jnp.concatenate(parts, axis=0)
    fetches[3].wait()
    taps = filters.shape[1]
    for first in range(0, taps, WIDE):
        block = jnp.dot(stacked, filters[:, first : first + WIDE], preferred_element_type=jnp.float32)
        for cut in range(cuts):
            bank_stage[cut, :, first : first + WIDE] = block[cut * share : (cut + 1) * share]
    banks = []
    for step in range(1, cuts):
        target = partner(me, step)
        banks.append(pltpu.make_async_remote_copy(
            src_ref=bank_stage.at[target], dst_ref=bank_at(step),
            send_sem=bank_send.at[step - 1], recv_sem=bank_recv.at[step - 1],
            device_id={"cuts": target}, device_id_type=MESH,
        ))
    for copy in banks:
        copy.start()

    pieces = taps // WIDE
    length = series.shape[2]
    window = length - taps
    chunks = length // LANES

    def fetch(step):
        return lambda det, at: series[step * dets + det, :, pl.ds(at, LANES)]

    full = batches_of(window // WIDE, pieces)
    short = batches_of(window // COARSEST // WIDE, pieces)

    def batches_at(step):
        return jnp.where(partner(me, step) == cuts - 1, short, full)

    def build(step, bank, between=None):
        convolve_building(
            stack(bank, pieces), fetch(step), everyone, pieces, chunks, batches_at(step),
            even, odd, last, partial_ref.at[step], between,
        )

    def sides(step):
        return side[step * (dets - 1) : (step + 1) * (dets - 1)]

    def forward(step):
        cross[step - 1].wait_recv()
        for copy in sides(step):
            copy.start()

    def forward_first():
        for step in range(1, early + 2):
            forward(step)

    everyone = list(range(dets))
    for copy in sides(0):
        copy.wait_recv()
    build(0, bank_stage[me], forward_first)
    for step in range(early + 2, cuts):
        forward(step)
    for step in range(early + 1, held + 1):
        fill(fetch(step), tiles_ref.at[step - early - 1], [core], chunks)
    for step in range(early + 1, held + 1):
        for copy in sides(step):
            copy.wait_recv()
        for turn in range(1, dets):
            fill(fetch(step), tiles_ref.at[step - early - 1], [lax.rem(core + turn, dets)], chunks)
    for step in range(1, early + 1):
        for copy in sides(step):
            copy.wait_recv()
        banks[step - 1].wait_recv()
        build(step, bank_early[step - 1])
    for copy in fetches[4:]:
        copy.wait()
    for copy in side[(held + 1) * (dets - 1) :]:
        copy.wait_recv()
    for copy in banks[early:]:
        copy.wait_recv()
    for copy in cross + side + banks:
        copy.wait_send()


def exchange(spans, strain, filters, weights, rates, delays, antenna, cuts, dets, early, ready):
    rows = weights.shape[0] // cuts // dets
    taps = filters.shape[1]
    length = strain.shape[-1]
    late = cuts - 1 - early
    rest = max(late - ready, 1)
    hbm = pl.BlockSpec(memory_space=pltpu.HBM)
    free = pl.BlockSpec(memory_space=pl.ANY)
    vmem = pl.BlockSpec(memory_space=pltpu.VMEM)
    dma = pltpu.SemaphoreType.DMA
    squares = (dets, tile_count(length, taps), LANES, LANES)
    return pl.pallas_call(
        functools.partial(exchange_kernel, cuts, dets, early, ready),
        out_shape=(
            jax.ShapeDtypeStruct((late, rows, taps), jnp.float32),
            jax.ShapeDtypeStruct((rest * dets, 1, length), jnp.float32),
            jax.ShapeDtypeStruct((1 + early, dets, total_tiles(length, taps), rows, LANES), jnp.float32),
            jax.ShapeDtypeStruct((ready, *squares), jnp.bfloat16),
            jax.ShapeDtypeStruct(rates.shape, rates.dtype),
            jax.ShapeDtypeStruct(delays.shape, delays.dtype),
            jax.ShapeDtypeStruct(antenna.shape, antenna.dtype),
        ),
        in_specs=[hbm] * 7,
        out_specs=(free, free, vmem, vmem, free, free, free),
        scratch_shapes=[
            pltpu.VMEM(spans.shape, spans.dtype),
            pltpu.VMEM(strain.shape, strain.dtype),
            pltpu.VMEM(weights.shape, weights.dtype),
            pltpu.VMEM(filters.shape, filters.dtype),
            pltpu.VMEM((cuts, rows, taps), jnp.float32),
            pltpu.VMEM((early, rows, taps), jnp.float32),
            pltpu.VMEM(((1 + early + ready) * dets, 1, length), jnp.float32),
            pltpu.VMEM((dets, BATCH + 1, LANES, LANES), jnp.bfloat16),
            pltpu.VMEM((dets, BATCH + 1, LANES, LANES), jnp.bfloat16),
            pltpu.VMEM((dets, LANES, LANES), jnp.bfloat16),
            dma((cuts - 1,)),
            dma((cuts - 1,)),
            dma((cuts - 1,)),
            dma((cuts - 1,)),
            dma((cuts * (dets - 1),)),
            dma((cuts * (dets - 1),)),
            dma((7,)),
        ],
        compiler_params=pltpu.CompilerParams(collective_id=0, has_side_effects=True, vmem_limit_bytes=GRANT),
    )(*[pltpu.with_memory_space_constraint(x, pltpu.HBM)
        for x in (spans, strain, weights, filters, rates, delays, antenna)])


def search_kernel(
    early, ready, rates_ref, delays_ref, antenna_ref, bank_ref, series_ref, partial_ref, tiles_ref, peak_ref,
    total, turned, best, *squares,
):
    late, rows, taps = bank_ref.shape
    dets = partial_ref.shape[1]
    window = peak_ref.shape[1]
    length = series_ref.shape[2]
    pieces = taps // WIDE
    skip = 2 * (pieces - 1)
    everyone = list(range(dets))
    me = lax.axis_index("cuts")

    groups = LANES // rows
    apart = window // LANES // groups
    span = apart * LANES
    split = max(1, COARSEST // apart)
    ways = groups // split
    group_at = [place % ways * split + place // ways for place in range(groups)]

    def level_of(step):
        rate = rates_ref[me ^ step]
        return sum((rate >= 2**known).astype(jnp.int32) for known in range(1, COARSEST.bit_length()))

    def filtered(index, tiles, level):
        blocks = lax.shift_right_logical(jnp.int32(window // WIDE), level)
        convolve(stack(bank_ref[index], pieces), tiles, everyone, pieces, batches_of(blocks, pieces), total)

    def widen(values, level):
        for known in range(COARSEST.bit_length()):
            @pl.when(level == known)
            def _(known=known):
                rate = 2**known
                per = apart // rate
                for det in range(dets):
                    blocks = []
                    for near in range(per):
                        block = jnp.concatenate(
                            [values[det, skip + group * per + near] for group in group_at], axis=0
                        )
                        blocks.append((near * LANES, block.T))
                    if not per:
                        block = jnp.concatenate([values[det, skip + way] for way in range(ways)], axis=0).T
                        part = LANES // split
                        blocks = [(0, jnp.concatenate(
                            [block[turn * part : (turn + 1) * part] for turn in range(split)], axis=1
                        ))]
                    for first, block in blocks:
                        size = block.shape[0]
                        for turn in range(rate):
                            if rate > 1:
                                place = pl.ds(first * rate + turn, size, stride=rate)
                            else:
                                place = pl.ds(first, size)
                            turned[det, place, :] += block

    for det in range(dets):
        turned[det] = jnp.zeros(turned.shape[1:], jnp.float32)
    for step in range(early + 1):
        widen(partial_ref.at[step], level_of(step))
    for index in range(ready):
        level = level_of(early + 1 + index)
        filtered(index, tiles_ref.at[index], level)
        widen(total, level)
    if late > ready:
        def one_slice(index, carry):
            level = level_of(early + 1 + index)
            fill(
                lambda det, at: series_ref[(index - ready) * dets + det, :, pl.ds(at, LANES)],
                squares[0], everyone, length // LANES,
            )
            filtered(index, squares[0], level)
            widen(total, level)
            return carry

        lax.fori_loop(ready, late, one_slice, 0)

    lane = lax.broadcasted_iota(jnp.int32, (HALO, LANES), 1)
    row, place = lane & (rows - 1), lane // rows
    group = (place & (ways - 1)) * split + place // ways
    later = jnp.minimum(group + 1, groups - 1)
    source = ((later & (split - 1)) * ways + later // split) * rows + row
    for det in range(dets):
        following = jnp.take_along_axis(turned[det, :HALO], source, axis=1)
        turned[det, span : span + HALO] = jnp.where(group == groups - 1, 0.0, following)

    for first in range(0, span, CHUNK):
        def direction(number, highest):
            summed = None
            for det in range(dets):
                start = delays_ref[det, number] + first
                term = antenna_ref[det, number] * turned[det, pl.ds(start, CHUNK), :]
                summed = term if summed is None else summed + term
            return jnp.maximum(highest, jnp.abs(summed))

        best[first : first + CHUNK] = lax.fori_loop(
            0, delays_ref.shape[1], direction, jnp.zeros((CHUNK, LANES), jnp.float32), unroll=16
        )
    for near in range(apart):
        back = best[near * LANES : (near + 1) * LANES].T
        for place, group in enumerate(group_at):
            at = (group * apart + near) * LANES
            peak_ref[:, at : at + LANES] = back[place * rows : (place + 1) * rows]


def search(rates, delays, antenna, bank, series, partial, tiles, window, early):
    late, rows, taps = bank.shape
    ready = tiles.shape[0]
    dets = partial.shape[1]
    span = window // (LANES // rows)
    smem = pl.BlockSpec(memory_space=pltpu.SMEM)
    vmem = pl.BlockSpec(memory_space=pltpu.VMEM)
    return pl.pallas_call(
        functools.partial(search_kernel, early, ready),
        out_shape=jax.ShapeDtypeStruct((rows, window), jnp.float32),
        in_specs=[smem, smem, smem, vmem, vmem, vmem, vmem],
        out_specs=vmem,
        scratch_shapes=[
            pltpu.VMEM(partial.shape[1:], jnp.float32),
            pltpu.VMEM((dets, span + HALO, LANES), jnp.float32),
            pltpu.VMEM((span, LANES), jnp.float32),
        ] + [pltpu.VMEM(tiles.shape[1:], tiles.dtype)] * (late > ready),
        compiler_params=pltpu.CompilerParams(vmem_limit_bytes=GRANT),
    )(rates, delays, antenna, bank, series, partial, tiles)


def shards(strain, filters, recon_weights, row_spans, slice_rates, delays, antenna):
    cuts = lax.axis_size("cuts")
    dets = lax.axis_size("det")
    early = min(EARLY, cuts - 2)
    ready = min(READY, cuts - 1 - early)
    bank, series, partial, tiles, rates, delays, antenna = exchange(
        row_spans.reshape(1, -1), strain.reshape(1, -1), filters[0], recon_weights[0],
        slice_rates, delays.T, antenna.T, cuts, dets, early, ready,
    )
    window = strain.shape[-1] - filters.shape[-1]
    return search(rates, delays, antenna, bank, series, partial, tiles, window, early)


def solution(mesh):
    placed = (
        P("cuts", "det", None),
        P(("bank", "cuts"), None, None),
        P(("bank", "cuts"), None, None),
        P("bank"),
        P(),
        P(),
        P(),
    )
    return jax.shard_map(
        shards,
        mesh=mesh,
        in_specs=placed,
        out_specs=P(("bank", "cuts", "det"), None),
        check_vma=False,
    )
```

```python
import functools

import jax
import jax.numpy as jnp
from jax import lax
from jax.experimental import pallas as pl
from jax.experimental.pallas import tpu as pltpu
from jax.sharding import PartitionSpec as P

MESH = pl.DeviceIdType.MESH
LANES = 128
WIDE = 256
BATCH = 12
DEEP = 48
COARSEST = 8
HALO = 48
CHUNK = 64
EARLY = 2
READY = 1
GRANT = 24 * 2**20


def partner(me, step):
    bit, other = 1, me
    while bit <= step:
        if step & bit:
            other = other + bit * (1 - 2 * lax.rem(lax.div(me, bit), 2))
        bit *= 2
    return other


def batches_of(blocks, pieces):
    return (blocks + pieces - 1 + BATCH - 1) // BATCH


def total_tiles(length, taps):
    pieces = taps // WIDE
    return 2 * (BATCH * batches_of((length - taps) // WIDE, pieces) + pieces - 1)


def tile_count(length, taps):
    return 2 * BATCH * batches_of((length - taps) // WIDE, taps // WIDE) + 2


def fill(fetch, tiles, dets, chunks):
    deep = next(deep for deep in range(DEEP, 0, -1) if chunks % deep == 0)
    ahead = lax.broadcasted_iota(jnp.int32, (LANES, LANES), 1) >= lax.broadcasted_iota(
        jnp.int32, (LANES, LANES), 0
    )

    def some(number, carry):
        left = []
        for det, before in zip(dets, carry):
            for near in range(deep):
                chunk = number * deep + near
                piece = fetch(det, pl.multiple_of(chunk * LANES, LANES))
                now = pltpu.roll(jnp.broadcast_to(piece, (LANES, LANES)), 0, 1, stride=1, stride_axis=0)
                tiles[det, chunk] = jnp.where(ahead, now, before).astype(jnp.bfloat16)
                before = now
            left.append(before)
        return tuple(left)

    lax.fori_loop(0, chunks // deep, some, tuple(jnp.zeros((LANES, LANES), jnp.float32) for det in dets))


def stack(bank, pieces):
    taps = bank.astype(jnp.bfloat16)
    return jnp.concatenate([taps[:, piece * WIDE : (piece + 1) * WIDE] for piece in range(pieces)], axis=0)


def convolve(stacked, tiles, dets, pieces, batches, total):
    rows = stacked.shape[0] // pieces

    def one_batch(batch, carry):
        base = BATCH * batch
        for det in dets:
            sums = [None] * (BATCH + pieces - 1)
            for near in range(BATCH):
                first = 2 * (base + near) + 1
                low, middle, high = tiles[det, first], tiles[det, first + 1], tiles[det, first + 2]
                square = jnp.concatenate(
                    [jnp.concatenate([middle, high], axis=1), jnp.concatenate([low, middle], axis=1)], axis=0
                )
                result = jnp.dot(stacked, square, preferred_element_type=jnp.float32)
                for piece in range(pieces):
                    term = result[piece * rows : (piece + 1) * rows]
                    old = sums[near + piece]
                    sums[near + piece] = term if old is None else old + term
            for far, value in enumerate(sums):
                for half in range(2):
                    at = 2 * (base + far) + half
                    part = value[:, half * LANES : (half + 1) * LANES]
                    total[det, at] = part if far >= pieces - 1 else total[det, at] + part
        return carry

    lax.fori_loop(0, batches, one_batch, 0)


def convolve_flat(stacked, tiles, dets, pieces, blocks, total):
    rows = stacked.shape[0] // pieces
    for det in dets:
        sums = [None] * blocks
        for near in range(blocks + pieces - 1):
            first = 2 * near + 1
            low, middle, high = tiles[det, first], tiles[det, first + 1], tiles[det, first + 2]
            square = jnp.concatenate(
                [jnp.concatenate([middle, high], axis=1), jnp.concatenate([low, middle], axis=1)], axis=0
            )
            result = jnp.dot(stacked, square, preferred_element_type=jnp.float32)
            for piece in range(pieces):
                block = near + piece - (pieces - 1)
                if 0 <= block < blocks:
                    term = result[piece * rows : (piece + 1) * rows]
                    sums[block] = term if sums[block] is None else sums[block] + term
        for block, value in enumerate(sums):
            for half in range(2):
                at = 2 * (pieces - 1 + block) + half
                total[det, at] = value[:, half * LANES : (half + 1) * LANES]


def exchange_kernel(
    cuts, dets, early, ready,
    spans_hbm, strain_hbm, weights_hbm, filters_hbm, rates_hbm, delays_hbm, antenna_hbm,
    bank_ref, series_ref, partial_ref, tiles_ref, rates_ref, delays_ref, antenna_ref,
    spans_ref, strain_ref, weights_ref, filters, bank_stage, bank_early, series, tiles,
    bank_send, bank_recv, cross_send, cross_recv, side_send, side_recv,
    local_sem,
):
    me = lax.axis_index("cuts")
    core = lax.axis_index("det")
    barrier = pltpu.get_barrier_semaphore()
    for step in range(1, cuts):
        pl.semaphore_signal(
            barrier, inc=1, device_id={"cuts": partner(me, step)}, device_id_type=MESH
        )
    for turn in range(1, dets):
        pl.semaphore_signal(
            barrier, inc=1, device_id={"det": lax.rem(core + turn, dets)}, device_id_type=MESH
        )

    fetches = [
        pltpu.make_async_copy(strain_hbm, strain_ref, local_sem.at[0]),
        pltpu.make_async_copy(spans_hbm, spans_ref, local_sem.at[1]),
        pltpu.make_async_copy(weights_hbm, weights_ref, local_sem.at[2]),
        pltpu.make_async_copy(filters_hbm, filters, local_sem.at[3]),
        pltpu.make_async_copy(rates_hbm, rates_ref, local_sem.at[4]),
        pltpu.make_async_copy(delays_hbm, delays_ref, local_sem.at[5]),
        pltpu.make_async_copy(antenna_hbm, antenna_ref, local_sem.at[6]),
    ]
    for copy in fetches:
        copy.start()
    held = early + ready

    def series_at(step, det):
        if step <= held:
            return series.at[step * dets + det]
        return series_ref.at[(step - held - 1) * dets + det]

    def bank_at(step):
        return bank_early.at[step - 1] if step <= early else bank_ref.at[step - early - 1]

    fetches[0].wait()
    series[core] = strain_ref[...].astype(jnp.float32)
    pl.semaphore_wait(barrier, cuts - 1 + dets - 1)
    cross = []
    for step in range(1, cuts):
        cross.append(pltpu.make_async_remote_copy(
            src_ref=series_at(0, core), dst_ref=series_at(step, core),
            send_sem=cross_send.at[step - 1], recv_sem=cross_recv.at[step - 1],
            device_id={"cuts": partner(me, step)}, device_id_type=MESH,
        ))
    side = []
    for step in range(cuts):
        for turn in range(1, dets):
            number = step * (dets - 1) + turn - 1
            side.append(pltpu.make_async_remote_copy(
                src_ref=series_at(step, core), dst_ref=series_at(step, core),
                send_sem=side_send.at[number], recv_sem=side_recv.at[number],
                device_id={"det": lax.rem(core + turn, dets)}, device_id_type=MESH,
            ))
    for copy in cross:
        copy.start()
    for copy in side[: dets - 1]:
        copy.start()

    fetches[1].wait()
    fetches[2].wait()
    rows = weights_ref.shape[0]
    share = rows // cuts // dets
    live = (me < spans_ref[...]).astype(jnp.float32)
    across = lax.broadcasted_iota(jnp.int32, (rows, rows), 1)
    down = lax.broadcasted_iota(jnp.int32, (rows, rows), 0)
    keep = jnp.sum(jnp.where(across == down, live, 0.0), axis=1, keepdims=True)
    kept = (weights_ref[...].astype(jnp.float32) * keep).astype(jnp.bfloat16)
    parts = []
    for cut in range(cuts):
        low = kept[(cut * dets) * share : (cut * dets + 1) * share]
        for det in range(1, dets):
            other = kept[(cut * dets + det) * share : (cut * dets + det + 1) * share]
            low = jnp.where(core == det, other, low)
        parts.append(low)
    stacked = jnp.concatenate(parts, axis=0)
    fetches[3].wait()
    taps = filters.shape[1]
    for first in range(0, taps, WIDE):
        block = jnp.dot(stacked, filters[:, first : first + WIDE], preferred_element_type=jnp.float32)
        for cut in range(cuts):
            bank_stage[cut, :, first : first + WIDE] = block[cut * share : (cut + 1) * share]
    banks = []
    for step in range(1, cuts):
        target = partner(me, step)
        banks.append(pltpu.make_async_remote_copy(
            src_ref=bank_stage.at[target], dst_ref=bank_at(step),
            send_sem=bank_send.at[step - 1], recv_sem=bank_recv.at[step - 1],
            device_id={"cuts": target}, device_id_type=MESH,
        ))
    for copy in banks:
        copy.start()

    pieces = taps // WIDE
    length = series.shape[2]
    window = length - taps
    chunks = length // LANES

    def fetch(step):
        return lambda det, at: series[step * dets + det, :, pl.ds(at, LANES)]

    full = batches_of(window // WIDE, pieces)
    short = batches_of(window // COARSEST // WIDE, pieces)

    def batches_at(step):
        return jnp.where(partner(me, step) == cuts - 1, short, full)

    def filtered(step, bank):
        out = tiles.at[step] if step <= early else tiles_ref.at[step - early - 1]
        convolve(stack(bank, pieces), out, everyone, pieces, batches_at(step), partial_ref.at[step])

    def prepare(step, det):
        out = tiles.at[step] if step <= early else tiles_ref.at[step - early - 1]
        fill(fetch(step), out, [det], chunks)

    def sides(step):
        return side[step * (dets - 1) : (step + 1) * (dets - 1)]

    def forward(step):
        cross[step - 1].wait_recv()
        for copy in sides(step):
            copy.start()

    def prepare_others(step):
        for copy in sides(step):
            copy.wait_recv()
        for turn in range(1, dets):
            prepare(step, lax.rem(core + turn, dets))

    everyone = list(range(dets))
    prepare(0, core)
    prepare_others(0)
    for step in range(1, early + 1):
        forward(step)
    filtered(0, bank_stage[me])
    for step in range(1, early + 1):
        prepare(step, core)
    for step in range(early + 1, cuts):
        forward(step)
    for step in range(early + 1, held + 1):
        prepare(step, core)
    for step in range(1, held + 1):
        prepare_others(step)
    for step in range(1, early + 1):
        banks[step - 1].wait_recv()
        filtered(step, bank_early[step - 1])
    for copy in fetches[4:]:
        copy.wait()
    for copy in side[(held + 1) * (dets - 1) :]:
        copy.wait_recv()
    for copy in banks[early:]:
        copy.wait_recv()
    for copy in cross + side + banks:
        copy.wait_send()


def exchange(spans, strain, filters, weights, rates, delays, antenna, cuts, dets, early, ready):
    rows = weights.shape[0] // cuts // dets
    taps = filters.shape[1]
    length = strain.shape[-1]
    late = cuts - 1 - early
    rest = max(late - ready, 1)
    hbm = pl.BlockSpec(memory_space=pltpu.HBM)
    free = pl.BlockSpec(memory_space=pl.ANY)
    vmem = pl.BlockSpec(memory_space=pltpu.VMEM)
    dma = pltpu.SemaphoreType.DMA
    squares = (dets, tile_count(length, taps), LANES, LANES)
    return pl.pallas_call(
        functools.partial(exchange_kernel, cuts, dets, early, ready),
        out_shape=(
            jax.ShapeDtypeStruct((late, rows, taps), jnp.float32),
            jax.ShapeDtypeStruct((rest * dets, 1, length), jnp.float32),
            jax.ShapeDtypeStruct((1 + early, dets, total_tiles(length, taps), rows, LANES), jnp.float32),
            jax.ShapeDtypeStruct((ready, *squares), jnp.bfloat16),
            jax.ShapeDtypeStruct(rates.shape, rates.dtype),
            jax.ShapeDtypeStruct(delays.shape, delays.dtype),
            jax.ShapeDtypeStruct(antenna.shape, antenna.dtype),
        ),
        in_specs=[hbm] * 7,
        out_specs=(free, free, vmem, vmem, free, free, free),
        scratch_shapes=[
            pltpu.VMEM(spans.shape, spans.dtype),
            pltpu.VMEM(strain.shape, strain.dtype),
            pltpu.VMEM(weights.shape, weights.dtype),
            pltpu.VMEM(filters.shape, filters.dtype),
            pltpu.VMEM((cuts, rows, taps), jnp.float32),
            pltpu.VMEM((early, rows, taps), jnp.float32),
            pltpu.VMEM(((1 + early + ready) * dets, 1, length), jnp.float32),
            pltpu.VMEM((1 + early, *squares), jnp.bfloat16),
            dma((cuts - 1,)),
            dma((cuts - 1,)),
            dma((cuts - 1,)),
            dma((cuts - 1,)),
            dma((cuts * (dets - 1),)),
            dma((cuts * (dets - 1),)),
            dma((7,)),
        ],
        compiler_params=pltpu.CompilerParams(collective_id=0, has_side_effects=True, vmem_limit_bytes=GRANT),
    )(*[pltpu.with_memory_space_constraint(x, pltpu.HBM)
        for x in (spans, strain, weights, filters, rates, delays, antenna)])


def search_kernel(
    early, ready, rates_ref, delays_ref, antenna_ref, bank_ref, series_ref, partial_ref, tiles_ref, peak_ref,
    total, turned, best, *squares,
):
    late, rows, taps = bank_ref.shape
    dets = partial_ref.shape[1]
    window = peak_ref.shape[1]
    length = series_ref.shape[2]
    pieces = taps // WIDE
    skip = 2 * (pieces - 1)
    everyone = list(range(dets))
    me = lax.axis_index("cuts")

    groups = LANES // rows
    apart = window // LANES // groups
    span = apart * LANES
    split = max(1, COARSEST // apart)
    ways = groups // split
    group_at = [place % ways * split + place // ways for place in range(groups)]

    def level_of(step):
        rate = rates_ref[me ^ step]
        return sum((rate >= 2**known).astype(jnp.int32) for known in range(1, COARSEST.bit_length()))

    def widen(values, known, fresh):
        rate = 2**known
        per = apart // rate
        for det in range(dets):
            blocks = []
            for near in range(per):
                block = jnp.concatenate(
                    [values[det, skip + group * per + near] for group in group_at], axis=0
                )
                blocks.append((near * LANES, block.T))
            if not per:
                block = jnp.concatenate([values[det, skip + way] for way in range(ways)], axis=0).T
                part = LANES // split
                blocks = [(0, jnp.concatenate(
                    [block[turn * part : (turn + 1) * part] for turn in range(split)], axis=1
                ))]
            for first, block in blocks:
                size = block.shape[0]
                for turn in range(rate):
                    if rate > 1:
                        place = pl.ds(first * rate + turn, size, stride=rate)
                    else:
                        place = pl.ds(first, size)
                    if fresh:
                        turned[det, place, :] = block
                    else:
                        turned[det, place, :] += block

    def by_level(level, work):
        for known in range(COARSEST.bit_length()):
            pl.when(level == known)(functools.partial(work, known))

    def one_slice(index, tiles):
        def work(known):
            blocks = window // WIDE // 2**known
            convolve_flat(stack(bank_ref[index], pieces), tiles, everyone, pieces, blocks, total)
            widen(total, known, False)

        by_level(level_of(early + 1 + index), work)

    for step in range(early + 1):
        by_level(level_of(step), functools.partial(widen, partial_ref.at[step], fresh=step == 0))
    for index in range(ready):
        one_slice(index, tiles_ref.at[index])
    if late > ready:
        def rest(index, carry):
            fill(
                lambda det, at: series_ref[(index - ready) * dets + det, :, pl.ds(at, LANES)],
                squares[0], everyone, length // LANES,
            )
            one_slice(index, squares[0])
            return carry

        lax.fori_loop(ready, late, rest, 0)

    lane = lax.broadcasted_iota(jnp.int32, (HALO, LANES), 1)
    row, place = lane & (rows - 1), lane // rows
    group = (place & (ways - 1)) * split + place // ways
    later = jnp.minimum(group + 1, groups - 1)
    source = ((later & (split - 1)) * ways + later // split) * rows + row
    for det in range(dets):
        following = jnp.take_along_axis(turned[det, :HALO], source, axis=1)
        turned[det, span : span + HALO] = jnp.where(group == groups - 1, 0.0, following)

    for first in range(0, span, CHUNK):
        def direction(number, highest):
            summed = None
            for det in range(dets):
                start = delays_ref[det, number] + first
                term = antenna_ref[det, number] * turned[det, pl.ds(start, CHUNK), :]
                summed = term if summed is None else summed + term
            return jnp.maximum(highest, jnp.abs(summed))

        best[first : first + CHUNK] = lax.fori_loop(
            0, delays_ref.shape[1], direction, jnp.zeros((CHUNK, LANES), jnp.float32), unroll=16
        )
    for near in range(apart):
        back = best[near * LANES : (near + 1) * LANES].T
        for place, group in enumerate(group_at):
            at = (group * apart + near) * LANES
            peak_ref[:, at : at + LANES] = back[place * rows : (place + 1) * rows]


def search(rates, delays, antenna, bank, series, partial, tiles, window, early):
    late, rows, taps = bank.shape
    ready = tiles.shape[0]
    dets = partial.shape[1]
    span = window // (LANES // rows)
    smem = pl.BlockSpec(memory_space=pltpu.SMEM)
    vmem = pl.BlockSpec(memory_space=pltpu.VMEM)
    return pl.pallas_call(
        functools.partial(search_kernel, early, ready),
        out_shape=jax.ShapeDtypeStruct((rows, window), jnp.float32),
        in_specs=[smem, smem, smem, vmem, vmem, vmem, vmem],
        out_specs=vmem,
        scratch_shapes=[
            pltpu.VMEM(partial.shape[1:], jnp.float32),
            pltpu.VMEM((dets, span + HALO, LANES), jnp.float32),
            pltpu.VMEM((span, LANES), jnp.float32),
        ] + [pltpu.VMEM(tiles.shape[1:], tiles.dtype)] * (late > ready),
        compiler_params=pltpu.CompilerParams(vmem_limit_bytes=GRANT),
    )(rates, delays, antenna, bank, series, partial, tiles)


def shards(strain, filters, recon_weights, row_spans, slice_rates, delays, antenna):
    cuts = lax.axis_size("cuts")
    dets = lax.axis_size("det")
    early = min(EARLY, cuts - 2)
    ready = min(READY, cuts - 1 - early)
    bank, series, partial, tiles, rates, delays, antenna = exchange(
        row_spans.reshape(1, -1), strain.reshape(1, -1), filters[0], recon_weights[0],
        slice_rates, delays.T, antenna.T, cuts, dets, early, ready,
    )
    window = strain.shape[-1] - filters.shape[-1]
    return search(rates, delays, antenna, bank, series, partial, tiles, window, early)


def solution(mesh):
    placed = (
        P("cuts", "det", None),
        P(("bank", "cuts"), None, None),
        P(("bank", "cuts"), None, None),
        P("bank"),
        P(),
        P(),
        P(),
    )
    return jax.shard_map(
        shards,
        mesh=mesh,
        in_specs=placed,
        out_specs=P(("bank", "cuts", "det"), None),
        check_vma=False,
    )
```

```python
import functools

import jax
import jax.numpy as jnp
from jax import lax
from jax.experimental import pallas as pl
from jax.experimental.pallas import tpu as pltpu
from jax.sharding import PartitionSpec as P

MESH = pl.DeviceIdType.MESH
LANES = 128
WIDE = 256
DEEP = 48
COARSEST = 8
HALO = 48
CHUNK = 64
EARLY = 2
READY = 1
GRANT = 24 * 2**20


def partner(me, step):
    bit, other = 1, me
    while bit <= step:
        if step & bit:
            other = other + bit * (1 - 2 * lax.rem(lax.div(me, bit), 2))
        bit *= 2
    return other


def tile_count(length):
    return length // LANES


def fill(fetch, tiles, dets, chunks):
    deep = next(deep for deep in range(DEEP, 0, -1) if chunks % deep == 0)
    ahead = lax.broadcasted_iota(jnp.int32, (LANES, LANES), 1) >= lax.broadcasted_iota(
        jnp.int32, (LANES, LANES), 0
    )

    def some(number, carry):
        left = []
        for det, before in zip(dets, carry):
            for near in range(deep):
                chunk = number * deep + near
                piece = fetch(det, pl.multiple_of(chunk * LANES, LANES))
                now = pltpu.roll(jnp.broadcast_to(piece, (LANES, LANES)), 0, 1, stride=1, stride_axis=0)
                tiles[det, chunk] = jnp.where(ahead, now, before).astype(jnp.bfloat16)
                before = now
            left.append(before)
        return tuple(left)

    lax.fori_loop(0, chunks // deep, some, tuple(jnp.zeros((LANES, LANES), jnp.float32) for det in dets))


def stack(bank, pieces):
    taps = bank.astype(jnp.bfloat16)
    return jnp.concatenate([taps[:, piece * WIDE : (piece + 1) * WIDE] for piece in range(pieces)], axis=0)


def convolve(stacked, tiles, dets, pieces, begin, end, blocks, total):
    rows = stacked.shape[0] // pieces
    for det in dets:
        sums = {}
        for near in range(begin, end):
            first = 2 * near + 1
            low, middle, high = tiles[det, first], tiles[det, first + 1], tiles[det, first + 2]
            square = jnp.concatenate(
                [jnp.concatenate([middle, high], axis=1), jnp.concatenate([low, middle], axis=1)], axis=0
            )
            result = jnp.dot(stacked, square, preferred_element_type=jnp.float32)
            for piece in range(pieces):
                block = near + piece - (pieces - 1)
                if 0 <= block < blocks:
                    term = result[piece * rows : (piece + 1) * rows]
                    sums[block] = sums[block] + term if block in sums else term
        for block, value in sums.items():
            for half in range(2):
                at = 2 * block + half
                part = value[:, half * LANES : (half + 1) * LANES]
                total[det, at] = part if begin <= block or not begin else total[det, at] + part


def exchange_kernel(
    cuts, dets, early, ready,
    spans_hbm, strain_hbm, weights_hbm, filters_hbm, rates_hbm, delays_hbm, antenna_hbm,
    bank_ref, series_ref, partial_ref, tiles_ref, rates_ref, delays_ref, antenna_ref,
    spans_ref, strain_ref, weights_ref, filters, bank_stage, bank_early, series, tiles,
    bank_send, bank_recv, cross_send, cross_recv, side_send, side_recv,
    local_sem,
):
    me = lax.axis_index("cuts")
    core = lax.axis_index("det")
    barrier = pltpu.get_barrier_semaphore()
    for step in range(1, cuts):
        pl.semaphore_signal(
            barrier, inc=1, device_id={"cuts": partner(me, step)}, device_id_type=MESH
        )
    for turn in range(1, dets):
        pl.semaphore_signal(
            barrier, inc=1, device_id={"det": lax.rem(core + turn, dets)}, device_id_type=MESH
        )

    fetches = [
        pltpu.make_async_copy(strain_hbm, strain_ref, local_sem.at[0]),
        pltpu.make_async_copy(spans_hbm, spans_ref, local_sem.at[1]),
        pltpu.make_async_copy(weights_hbm, weights_ref, local_sem.at[2]),
        pltpu.make_async_copy(filters_hbm, filters, local_sem.at[3]),
        pltpu.make_async_copy(rates_hbm, rates_ref, local_sem.at[4]),
        pltpu.make_async_copy(delays_hbm, delays_ref, local_sem.at[5]),
        pltpu.make_async_copy(antenna_hbm, antenna_ref, local_sem.at[6]),
    ]
    for copy in fetches:
        copy.start()
    held = early + ready

    def series_at(step, det):
        if step <= held:
            return series.at[step * dets + det]
        return series_ref.at[(step - held - 1) * dets + det]

    def bank_at(step):
        return bank_early.at[step - 1] if step <= early else bank_ref.at[step - early - 1]

    fetches[0].wait()
    series[core] = strain_ref[...].astype(jnp.float32)
    pl.semaphore_wait(barrier, cuts - 1 + dets - 1)
    cross = []
    for step in range(1, cuts):
        cross.append(pltpu.make_async_remote_copy(
            src_ref=series_at(0, core), dst_ref=series_at(step, core),
            send_sem=cross_send.at[step - 1], recv_sem=cross_recv.at[step - 1],
            device_id={"cuts": partner(me, step)}, device_id_type=MESH,
        ))
    side = []
    for step in range(cuts):
        for turn in range(1, dets):
            number = step * (dets - 1) + turn - 1
            side.append(pltpu.make_async_remote_copy(
                src_ref=series_at(step, core), dst_ref=series_at(step, core),
                send_sem=side_send.at[number], recv_sem=side_recv.at[number],
                device_id={"det": lax.rem(core + turn, dets)}, device_id_type=MESH,
            ))
    for copy in cross:
        copy.start()
    for copy in side[: dets - 1]:
        copy.start()

    fetches[1].wait()
    fetches[2].wait()
    rows = weights_ref.shape[0]
    share = rows // cuts // dets
    live = (me < spans_ref[...]).astype(jnp.float32)
    across = lax.broadcasted_iota(jnp.int32, (rows, rows), 1)
    down = lax.broadcasted_iota(jnp.int32, (rows, rows), 0)
    keep = jnp.sum(jnp.where(across == down, live, 0.0), axis=1, keepdims=True)
    kept = (weights_ref[...].astype(jnp.float32) * keep).astype(jnp.bfloat16)
    parts = []
    for cut in range(cuts):
        low = kept[(cut * dets) * share : (cut * dets + 1) * share]
        for det in range(1, dets):
            other = kept[(cut * dets + det) * share : (cut * dets + det + 1) * share]
            low = jnp.where(core == det, other, low)
        parts.append(low)
    stacked = jnp.concatenate(parts, axis=0)
    fetches[3].wait()
    taps = filters.shape[1]
    for first in range(0, taps, WIDE):
        block = jnp.dot(stacked, filters[:, first : first + WIDE], preferred_element_type=jnp.float32)
        for cut in range(cuts):
            bank_stage[cut, :, first : first + WIDE] = block[cut * share : (cut + 1) * share]
    banks = []
    for step in range(1, cuts):
        target = partner(me, step)
        banks.append(pltpu.make_async_remote_copy(
            src_ref=bank_stage.at[target], dst_ref=bank_at(step),
            send_sem=bank_send.at[step - 1], recv_sem=bank_recv.at[step - 1],
            device_id={"cuts": target}, device_id_type=MESH,
        ))
    for copy in banks:
        copy.start()

    pieces = taps // WIDE
    length = series.shape[2]
    window = length - taps
    chunks = length // LANES

    def fetch(step):
        return lambda det, at: series[step * dets + det, :, pl.ds(at, LANES)]

    def filtered(step, bank):
        out = tiles.at[step] if step <= early else tiles_ref.at[step - early - 1]
        coarse = partner(me, step) == cuts - 1

        def work(samples):
            convolve(stack(bank, pieces), out, everyone, pieces, 0, samples // WIDE + pieces - 1, samples // WIDE,
                     partial_ref.at[step])

        pl.when(coarse)(functools.partial(work, window // COARSEST))
        pl.when(jnp.logical_not(coarse))(functools.partial(work, window))

    def prepare(step, det):
        out = tiles.at[step] if step <= early else tiles_ref.at[step - early - 1]
        fill(fetch(step), out, [det], chunks)

    def sides(step):
        return side[step * (dets - 1) : (step + 1) * (dets - 1)]

    def forward(step):
        cross[step - 1].wait_recv()
        for copy in sides(step):
            copy.start()

    def prepare_others(step):
        for copy in sides(step):
            copy.wait_recv()
        for turn in range(1, dets):
            prepare(step, lax.rem(core + turn, dets))

    everyone = list(range(dets))
    prepare(0, core)
    prepare_others(0)
    for step in range(1, early + 1):
        forward(step)
    filtered(0, bank_stage[me])
    for step in range(1, early + 1):
        prepare(step, core)
    for step in range(early + 1, cuts):
        forward(step)
    for step in range(early + 1, held + 1):
        prepare(step, core)
    for step in range(1, held + 1):
        prepare_others(step)
    for step in range(1, early + 1):
        banks[step - 1].wait_recv()
        filtered(step, bank_early[step - 1])
    for copy in fetches[4:]:
        copy.wait()
    for copy in side[(held + 1) * (dets - 1) :]:
        copy.wait_recv()
    for copy in banks[early:]:
        copy.wait_recv()
    for copy in cross + side + banks:
        copy.wait_send()


def exchange(spans, strain, filters, weights, rates, delays, antenna, cuts, dets, early, ready):
    rows = weights.shape[0] // cuts // dets
    taps = filters.shape[1]
    length = strain.shape[-1]
    late = cuts - 1 - early
    rest = max(late - ready, 1)
    hbm = pl.BlockSpec(memory_space=pltpu.HBM)
    free = pl.BlockSpec(memory_space=pl.ANY)
    vmem = pl.BlockSpec(memory_space=pltpu.VMEM)
    dma = pltpu.SemaphoreType.DMA
    squares = (dets, tile_count(length), LANES, LANES)
    return pl.pallas_call(
        functools.partial(exchange_kernel, cuts, dets, early, ready),
        out_shape=(
            jax.ShapeDtypeStruct((late, rows, taps), jnp.float32),
            jax.ShapeDtypeStruct((rest * dets, 1, length), jnp.float32),
            jax.ShapeDtypeStruct((1 + early, dets, (length - taps) // LANES, rows, LANES), jnp.float32),
            jax.ShapeDtypeStruct((ready, *squares), jnp.bfloat16),
            jax.ShapeDtypeStruct(rates.shape, rates.dtype),
            jax.ShapeDtypeStruct(delays.shape, delays.dtype),
            jax.ShapeDtypeStruct(antenna.shape, antenna.dtype),
        ),
        in_specs=[hbm] * 7,
        out_specs=(free, free, vmem, vmem, free, free, free),
        scratch_shapes=[
            pltpu.VMEM(spans.shape, spans.dtype),
            pltpu.VMEM(strain.shape, strain.dtype),
            pltpu.VMEM(weights.shape, weights.dtype),
            pltpu.VMEM(filters.shape, filters.dtype),
            pltpu.VMEM((cuts, rows, taps), jnp.float32),
            pltpu.VMEM((early, rows, taps), jnp.float32),
            pltpu.VMEM(((1 + early + ready) * dets, 1, length), jnp.float32),
            pltpu.VMEM((1 + early, *squares), jnp.bfloat16),
            dma((cuts - 1,)),
            dma((cuts - 1,)),
            dma((cuts - 1,)),
            dma((cuts - 1,)),
            dma((cuts * (dets - 1),)),
            dma((cuts * (dets - 1),)),
            dma((7,)),
        ],
        compiler_params=pltpu.CompilerParams(collective_id=0, has_side_effects=True, vmem_limit_bytes=GRANT),
    )(*[pltpu.with_memory_space_constraint(x, pltpu.HBM)
        for x in (spans, strain, weights, filters, rates, delays, antenna)])


def search_kernel(
    early, ready, rates_any, delays_any, antenna_any, bank_ref, series_ref, partial_ref, tiles_ref, peak_ref,
    rates_ref, delays_ref, antenna_ref, total, turned, best, table_sem, *squares,
):
    tables = [
        pltpu.make_async_copy(rates_any, rates_ref, table_sem.at[0]),
        pltpu.make_async_copy(delays_any, delays_ref, table_sem.at[1]),
        pltpu.make_async_copy(antenna_any, antenna_ref, table_sem.at[2]),
    ]
    for copy in tables:
        copy.start()
    late, rows, taps = bank_ref.shape
    dets = partial_ref.shape[1]
    window = peak_ref.shape[1]
    length = series_ref.shape[2]
    pieces = taps // WIDE
    everyone = list(range(dets))
    me = lax.axis_index("cuts")

    groups = LANES // rows
    apart = window // LANES // groups
    span = apart * LANES
    split = max(1, COARSEST // apart)
    ways = groups // split
    group_at = [place % ways * split + place // ways for place in range(groups)]

    def level_of(step):
        rate = rates_ref[me ^ step]
        return sum((rate >= 2**known).astype(jnp.int32) for known in range(1, COARSEST.bit_length()))

    def widen(values, known, fresh):
        rate = 2**known
        per = apart // rate
        for det in range(dets):
            blocks = []
            for near in range(per):
                block = jnp.concatenate(
                    [values[det, group * per + near] for group in group_at], axis=0
                )
                blocks.append((near * LANES, block.T))
            if not per:
                block = jnp.concatenate([values[det, way] for way in range(ways)], axis=0).T
                part = LANES // split
                blocks = [(0, jnp.concatenate(
                    [block[turn * part : (turn + 1) * part] for turn in range(split)], axis=1
                ))]
            for first, block in blocks:
                size = block.shape[0]
                for turn in range(rate):
                    if rate > 1:
                        place = pl.ds(first * rate + turn, size, stride=rate)
                    else:
                        place = pl.ds(first, size)
                    if fresh:
                        turned[det, place, :] = block
                    else:
                        turned[det, place, :] += block

    def by_level(level, work):
        for known in range(COARSEST.bit_length()):
            pl.when(level == known)(functools.partial(work, known))

    fewest = window // WIDE // COARSEST + pieces - 1

    def begin_slice(index, tiles):
        convolve(stack(bank_ref[index], pieces), tiles, everyone, pieces, 0, fewest, window // WIDE, total)

    def end_slice(index, tiles):
        def work(known):
            blocks = window // WIDE // 2**known
            convolve(
                stack(bank_ref[index], pieces), tiles, everyone, pieces, fewest, blocks + pieces - 1, blocks, total
            )
            widen(total, known, False)

        by_level(level_of(early + 1 + index), work)

    begin_slice(0, tiles_ref.at[0])
    for copy in tables:
        copy.wait()
    for step in range(early + 1):
        by_level(level_of(step), functools.partial(widen, partial_ref.at[step], fresh=step == 0))
    end_slice(0, tiles_ref.at[0])
    for index in range(1, ready):
        begin_slice(index, tiles_ref.at[index])
        end_slice(index, tiles_ref.at[index])
    if late > ready:
        def rest(index, carry):
            fill(
                lambda det, at: series_ref[(index - ready) * dets + det, :, pl.ds(at, LANES)],
                squares[0], everyone, length // LANES,
            )
            begin_slice(index, squares[0])
            end_slice(index, squares[0])
            return carry

        lax.fori_loop(ready, late, rest, 0)

    lane = lax.broadcasted_iota(jnp.int32, (HALO, LANES), 1)
    row, place = lane & (rows - 1), lane // rows
    group = (place & (ways - 1)) * split + place // ways
    later = jnp.minimum(group + 1, groups - 1)
    source = ((later & (split - 1)) * ways + later // split) * rows + row
    for det in range(dets):
        following = jnp.take_along_axis(turned[det, :HALO], source, axis=1)
        turned[det, span : span + HALO] = jnp.where(group == groups - 1, 0.0, following)

    for first in range(0, span, CHUNK):
        def direction(number, highest):
            summed = None
            for det in range(dets):
                start = delays_ref[det, number] + first
                term = antenna_ref[det, number] * turned[det, pl.ds(start, CHUNK), :]
                summed = term if summed is None else summed + term
            return jnp.maximum(highest, jnp.abs(summed))

        best[first : first + CHUNK] = lax.fori_loop(
            0, delays_ref.shape[1], direction, jnp.zeros((CHUNK, LANES), jnp.float32), unroll=32
        )
    for near in range(apart):
        back = best[near * LANES : (near + 1) * LANES].T
        for place, group in enumerate(group_at):
            at = (group * apart + near) * LANES
            peak_ref[:, at : at + LANES] = back[place * rows : (place + 1) * rows]


def search(rates, delays, antenna, bank, series, partial, tiles, window, early):
    late, rows, taps = bank.shape
    ready = tiles.shape[0]
    dets = partial.shape[1]
    span = window // (LANES // rows)
    free = pl.BlockSpec(memory_space=pl.ANY)
    vmem = pl.BlockSpec(memory_space=pltpu.VMEM)
    return pl.pallas_call(
        functools.partial(search_kernel, early, ready),
        out_shape=jax.ShapeDtypeStruct((rows, window), jnp.float32),
        in_specs=[free, free, free, vmem, vmem, vmem, vmem],
        out_specs=vmem,
        scratch_shapes=[
            pltpu.SMEM(rates.shape, rates.dtype),
            pltpu.SMEM(delays.shape, delays.dtype),
            pltpu.SMEM(antenna.shape, antenna.dtype),
            pltpu.VMEM(partial.shape[1:], jnp.float32),
            pltpu.VMEM((dets, span + HALO, LANES), jnp.float32),
            pltpu.VMEM((span, LANES), jnp.float32),
            pltpu.SemaphoreType.DMA((3,)),
        ] + [pltpu.VMEM(tiles.shape[1:], tiles.dtype)] * (late > ready),
        compiler_params=pltpu.CompilerParams(vmem_limit_bytes=GRANT),
    )(rates, delays, antenna, bank, series, partial, tiles)


def shards(strain, filters, recon_weights, row_spans, slice_rates, delays, antenna):
    cuts = lax.axis_size("cuts")
    dets = lax.axis_size("det")
    early = min(EARLY, cuts - 2)
    ready = min(READY, cuts - 1 - early)
    bank, series, partial, tiles, rates, delays, antenna = exchange(
        row_spans.reshape(1, -1), strain.reshape(1, -1), filters[0], recon_weights[0],
        slice_rates, delays.T, antenna.T, cuts, dets, early, ready,
    )
    window = strain.shape[-1] - filters.shape[-1]
    return search(rates, delays, antenna, bank, series, partial, tiles, window, early)


def solution(mesh):
    placed = (
        P("cuts", "det", None),
        P(("bank", "cuts"), None, None),
        P(("bank", "cuts"), None, None),
        P("bank"),
        P(),
        P(),
        P(),
    )
    return jax.shard_map(
        shards,
        mesh=mesh,
        in_specs=placed,
        out_specs=P(("bank", "cuts", "det"), None),
        check_vma=False,
    )
```

```python
import functools

import jax
import jax.numpy as jnp
from jax import lax
from jax.experimental import pallas as pl
from jax.experimental.pallas import tpu as pltpu
from jax.sharding import PartitionSpec as P

MESH = pl.DeviceIdType.MESH
LANES = 128
SUBLANES = 8
WIDE = 256
DEEP = 48
COARSEST = 8
HALO = 48
CHUNK = 64
EARLY = 2
READY = 1
GRANT = 24 * 2**20


def partner(me, step):
    bit, other = 1, me
    while bit <= step:
        if step & bit:
            other = other + bit * (1 - 2 * lax.rem(lax.div(me, bit), 2))
        bit *= 2
    return other


def tile_count(length):
    return length // LANES


def fill(fetch, tiles, dets, chunks):
    deep = next(deep for deep in range(DEEP, 0, -1) if chunks % deep == 0)
    ahead = lax.broadcasted_iota(jnp.int32, (LANES, LANES), 1) >= lax.broadcasted_iota(
        jnp.int32, (LANES, LANES), 0
    )

    def some(number, carry):
        left = []
        for det, before in zip(dets, carry):
            for near in range(deep):
                chunk = number * deep + near
                piece = fetch(det, pl.multiple_of(chunk * LANES, LANES))
                now = pltpu.roll(jnp.broadcast_to(piece, (LANES, LANES)), 0, 1, stride=1, stride_axis=0)
                tiles[det, chunk] = jnp.where(ahead, now, before).astype(jnp.bfloat16)
                before = now
            left.append(before)
        return tuple(left)

    lax.fori_loop(0, chunks // deep, some, tuple(jnp.zeros((LANES, LANES), jnp.float32) for det in dets))


def stack(bank, pieces):
    taps = bank.astype(jnp.bfloat16)
    return jnp.concatenate([taps[:, piece * WIDE : (piece + 1) * WIDE] for piece in range(pieces)], axis=0)


def convolve(stacked, tiles, dets, pieces, begin, end, blocks, total):
    rows = stacked.shape[0] // pieces
    for det in dets:
        sums = {}
        for near in range(begin, end):
            first = 2 * near + 1
            low, middle, high = tiles[det, first], tiles[det, first + 1], tiles[det, first + 2]
            square = jnp.concatenate(
                [jnp.concatenate([middle, high], axis=1), jnp.concatenate([low, middle], axis=1)], axis=0
            )
            result = jnp.dot(stacked, square, preferred_element_type=jnp.float32)
            for piece in range(pieces):
                block = near + piece - (pieces - 1)
                if 0 <= block < blocks:
                    term = result[piece * rows : (piece + 1) * rows]
                    sums[block] = sums[block] + term if block in sums else term
        for block, value in sums.items():
            for half in range(2):
                at = 2 * block + half
                part = value[:, half * LANES : (half + 1) * LANES]
                total[det, at] = part if begin <= block or not begin else total[det, at] + part


def exchange_kernel(
    cuts, dets, early, ready,
    spans_hbm, strain_hbm, weights_hbm, filters_hbm, rates_hbm, delays_hbm, antenna_hbm,
    bank_ref, series_ref, partial_ref, tiles_ref, rates_ref, delays_ref, antenna_ref,
    spans_ref, strain_ref, weights_ref, filters, bank_stage, bank_early, series, tiles,
    bank_send, bank_recv, cross_send, cross_recv, side_send, side_recv,
    local_sem,
):
    me = lax.axis_index("cuts")
    core = lax.axis_index("det")
    barrier = pltpu.get_barrier_semaphore()
    for step in range(1, cuts):
        pl.semaphore_signal(
            barrier, inc=1, device_id={"cuts": partner(me, step)}, device_id_type=MESH
        )
    for turn in range(1, dets):
        pl.semaphore_signal(
            barrier, inc=1, device_id={"det": lax.rem(core + turn, dets)}, device_id_type=MESH
        )

    fetches = [
        pltpu.make_async_copy(strain_hbm, strain_ref, local_sem.at[0]),
        pltpu.make_async_copy(spans_hbm, spans_ref, local_sem.at[1]),
        pltpu.make_async_copy(weights_hbm, weights_ref, local_sem.at[2]),
        pltpu.make_async_copy(filters_hbm, filters, local_sem.at[3]),
        pltpu.make_async_copy(rates_hbm, rates_ref, local_sem.at[4]),
        pltpu.make_async_copy(delays_hbm, delays_ref, local_sem.at[5]),
        pltpu.make_async_copy(antenna_hbm, antenna_ref, local_sem.at[6]),
    ]
    for copy in fetches:
        copy.start()
    held = early + ready

    def series_at(step, det):
        if step <= held:
            return series.at[step * dets + det]
        return series_ref.at[(step - held - 1) * dets + det]

    def bank_at(step):
        return bank_early.at[step - 1] if step <= early else bank_ref.at[step - early - 1]

    fetches[0].wait()
    series[core] = strain_ref[...].astype(jnp.float32)
    pl.semaphore_wait(barrier, cuts - 1 + dets - 1)
    cross = []
    for step in range(1, cuts):
        cross.append(pltpu.make_async_remote_copy(
            src_ref=series_at(0, core), dst_ref=series_at(step, core),
            send_sem=cross_send.at[step - 1], recv_sem=cross_recv.at[step - 1],
            device_id={"cuts": partner(me, step)}, device_id_type=MESH,
        ))
    side = []
    for step in range(cuts):
        for turn in range(1, dets):
            number = step * (dets - 1) + turn - 1
            side.append(pltpu.make_async_remote_copy(
                src_ref=series_at(step, core), dst_ref=series_at(step, core),
                send_sem=side_send.at[number], recv_sem=side_recv.at[number],
                device_id={"det": lax.rem(core + turn, dets)}, device_id_type=MESH,
            ))
    for copy in cross:
        copy.start()
    for copy in side[: dets - 1]:
        copy.start()

    fetches[1].wait()
    fetches[2].wait()
    rows = weights_ref.shape[0]
    share = rows // cuts // dets
    live = (me < spans_ref[...]).astype(jnp.float32)
    across = lax.broadcasted_iota(jnp.int32, (rows, rows), 1)
    down = lax.broadcasted_iota(jnp.int32, (rows, rows), 0)
    keep = jnp.sum(jnp.where(across == down, live, 0.0), axis=1, keepdims=True)
    kept = (weights_ref[...].astype(jnp.float32) * keep).astype(jnp.bfloat16)
    parts = []
    for cut in range(cuts):
        low = kept[(cut * dets) * share : (cut * dets + 1) * share]
        for det in range(1, dets):
            other = kept[(cut * dets + det) * share : (cut * dets + det + 1) * share]
            low = jnp.where(core == det, other, low)
        parts.append(low)
    stacked = jnp.concatenate(parts, axis=0)
    fetches[3].wait()
    taps = filters.shape[1]
    for first in range(0, taps, WIDE):
        block = jnp.dot(stacked, filters[:, first : first + WIDE], preferred_element_type=jnp.float32)
        for cut in range(cuts):
            bank_stage[cut, :, first : first + WIDE] = block[cut * share : (cut + 1) * share]
    banks = []
    for step in range(1, cuts):
        target = partner(me, step)
        banks.append(pltpu.make_async_remote_copy(
            src_ref=bank_stage.at[target], dst_ref=bank_at(step),
            send_sem=bank_send.at[step - 1], recv_sem=bank_recv.at[step - 1],
            device_id={"cuts": target}, device_id_type=MESH,
        ))
    for copy in banks:
        copy.start()

    pieces = taps // WIDE
    length = series.shape[2]
    window = length - taps
    chunks = length // LANES

    def fetch(step):
        return lambda det, at: series[step * dets + det, :, pl.ds(at, LANES)]

    def filtered(step, bank):
        out = tiles.at[step] if step <= early else tiles_ref.at[step - early - 1]
        coarse = partner(me, step) == cuts - 1

        def work(samples):
            convolve(stack(bank, pieces), out, everyone, pieces, 0, samples // WIDE + pieces - 1, samples // WIDE,
                     partial_ref.at[step])

        pl.when(coarse)(functools.partial(work, window // COARSEST))
        pl.when(jnp.logical_not(coarse))(functools.partial(work, window))

    def prepare(step, det):
        out = tiles.at[step] if step <= early else tiles_ref.at[step - early - 1]
        fill(fetch(step), out, [det], chunks)

    def sides(step):
        return side[step * (dets - 1) : (step + 1) * (dets - 1)]

    def forward(step):
        cross[step - 1].wait_recv()
        for copy in sides(step):
            copy.start()

    def prepare_others(step):
        for copy in sides(step):
            copy.wait_recv()
        for turn in range(1, dets):
            prepare(step, lax.rem(core + turn, dets))

    everyone = list(range(dets))
    prepare(0, core)
    prepare_others(0)
    for step in range(1, early + 1):
        forward(step)
    filtered(0, bank_stage[me])
    for step in range(1, early + 1):
        prepare(step, core)
    for step in range(early + 1, cuts):
        forward(step)
    for step in range(early + 1, held + 1):
        prepare(step, core)
    for step in range(1, early + 1):
        prepare_others(step)
    for step in range(1, early + 1):
        banks[step - 1].wait_recv()
        filtered(step, bank_early[step - 1])
        if step == 1:
            for late in range(early + 1, held + 1):
                prepare_others(late)
    for copy in fetches[4:]:
        copy.wait()
    for copy in side[(held + 1) * (dets - 1) :]:
        copy.wait_recv()
    for copy in banks[early:]:
        copy.wait_recv()
    for copy in cross + side + banks:
        copy.wait_send()


def exchange(spans, strain, filters, weights, rates, delays, antenna, cuts, dets, early, ready):
    rows = weights.shape[0] // cuts // dets
    taps = filters.shape[1]
    length = strain.shape[-1]
    late = cuts - 1 - early
    rest = max(late - ready, 1)
    hbm = pl.BlockSpec(memory_space=pltpu.HBM)
    free = pl.BlockSpec(memory_space=pl.ANY)
    vmem = pl.BlockSpec(memory_space=pltpu.VMEM)
    dma = pltpu.SemaphoreType.DMA
    squares = (dets, tile_count(length), LANES, LANES)
    return pl.pallas_call(
        functools.partial(exchange_kernel, cuts, dets, early, ready),
        out_shape=(
            jax.ShapeDtypeStruct((late, rows, taps), jnp.float32),
            jax.ShapeDtypeStruct((rest * dets, 1, length), jnp.float32),
            jax.ShapeDtypeStruct((1 + early, dets, (length - taps) // LANES, rows, LANES), jnp.float32),
            jax.ShapeDtypeStruct((ready, *squares), jnp.bfloat16),
            jax.ShapeDtypeStruct(rates.shape, rates.dtype),
            jax.ShapeDtypeStruct(delays.shape, delays.dtype),
            jax.ShapeDtypeStruct(antenna.shape, antenna.dtype),
        ),
        in_specs=[hbm] * 7,
        out_specs=(free, free, vmem, vmem, free, free, free),
        scratch_shapes=[
            pltpu.VMEM(spans.shape, spans.dtype),
            pltpu.VMEM(strain.shape, strain.dtype),
            pltpu.VMEM(weights.shape, weights.dtype),
            pltpu.VMEM(filters.shape, filters.dtype),
            pltpu.VMEM((cuts, rows, taps), jnp.float32),
            pltpu.VMEM((early, rows, taps), jnp.float32),
            pltpu.VMEM(((1 + early + ready) * dets, 1, length), jnp.float32),
            pltpu.VMEM((1 + early, *squares), jnp.bfloat16),
            dma((cuts - 1,)),
            dma((cuts - 1,)),
            dma((cuts - 1,)),
            dma((cuts - 1,)),
            dma((cuts * (dets - 1),)),
            dma((cuts * (dets - 1),)),
            dma((7,)),
        ],
        compiler_params=pltpu.CompilerParams(collective_id=0, has_side_effects=True, vmem_limit_bytes=GRANT),
    )(*[pltpu.with_memory_space_constraint(x, pltpu.HBM)
        for x in (spans, strain, weights, filters, rates, delays, antenna)])


def search_kernel(
    early, ready, rates_any, delays_any, antenna_any, bank_ref, series_ref, partial_ref, tiles_ref, peak_ref,
    rates_ref, delays_ref, antenna_ref, total, turned, spread, best, table_sem, *squares,
):
    tables = [
        pltpu.make_async_copy(rates_any, rates_ref, table_sem.at[0]),
        pltpu.make_async_copy(delays_any, delays_ref, table_sem.at[1]),
        pltpu.make_async_copy(antenna_any, antenna_ref, table_sem.at[2]),
    ]
    for copy in tables:
        copy.start()
    late, rows, taps = bank_ref.shape
    dets = partial_ref.shape[1]
    window = peak_ref.shape[1]
    length = series_ref.shape[2]
    pieces = taps // WIDE
    everyone = list(range(dets))
    me = lax.axis_index("cuts")

    groups = LANES // rows
    apart = window // LANES // groups
    span = apart * LANES
    split = max(1, COARSEST // apart)
    ways = groups // split
    group_at = [place % ways * split + place // ways for place in range(groups)]

    def level_of(step):
        rate = rates_ref[me ^ step]
        return sum((rate >= 2**known).astype(jnp.int32) for known in range(1, COARSEST.bit_length()))

    def widen(values, known, fresh):
        rate = 2**known
        per = apart // rate
        for det in range(dets):
            blocks = []
            for near in range(per):
                block = jnp.concatenate(
                    [values[det, group * per + near] for group in group_at], axis=0
                )
                blocks.append((near * LANES, block.T))
            if not per:
                block = jnp.concatenate([values[det, way] for way in range(ways)], axis=0).T
                part = LANES // split
                blocks = [(0, jnp.concatenate(
                    [block[turn * part : (turn + 1) * part] for turn in range(split)], axis=1
                ))]
            for first, block in blocks:
                size = block.shape[0]
                if rate == SUBLANES:
                    spread[det, :size] = block
                    for row in range(size):
                        place = pl.ds((first + row) * rate, rate)
                        value = jnp.broadcast_to(spread[det, row : row + 1], (rate, LANES))
                        turned[det, place, :] = value if fresh else turned[det, place, :] + value
                    continue
                for turn in range(rate):
                    if rate > 1:
                        place = pl.ds(first * rate + turn, size, stride=rate)
                    else:
                        place = pl.ds(first, size)
                    if fresh:
                        turned[det, place, :] = block
                    else:
                        turned[det, place, :] += block

    def by_level(level, work):
        for known in range(COARSEST.bit_length()):
            pl.when(level == known)(functools.partial(work, known))

    fewest = window // WIDE // COARSEST + pieces - 1

    def begin_slice(index, tiles):
        convolve(stack(bank_ref[index], pieces), tiles, everyone, pieces, 0, fewest, window // WIDE, total)

    def end_slice(index, tiles):
        def work(known):
            blocks = window // WIDE // 2**known
            convolve(
                stack(bank_ref[index], pieces), tiles, everyone, pieces, fewest, blocks + pieces - 1, blocks, total
            )
            widen(total, known, False)

        by_level(level_of(early + 1 + index), work)

    begin_slice(0, tiles_ref.at[0])
    for copy in tables:
        copy.wait()
    for step in range(early + 1):
        by_level(level_of(step), functools.partial(widen, partial_ref.at[step], fresh=step == 0))
    end_slice(0, tiles_ref.at[0])
    for index in range(1, ready):
        begin_slice(index, tiles_ref.at[index])
        end_slice(index, tiles_ref.at[index])
    if late > ready:
        def rest(index, carry):
            fill(
                lambda det, at: series_ref[(index - ready) * dets + det, :, pl.ds(at, LANES)],
                squares[0], everyone, length // LANES,
            )
            begin_slice(index, squares[0])
            end_slice(index, squares[0])
            return carry

        lax.fori_loop(ready, late, rest, 0)

    lane = lax.broadcasted_iota(jnp.int32, (HALO, LANES), 1)
    row, place = lane & (rows - 1), lane // rows
    group = (place & (ways - 1)) * split + place // ways
    later = jnp.minimum(group + 1, groups - 1)
    source = ((later & (split - 1)) * ways + later // split) * rows + row
    for det in range(dets):
        following = jnp.take_along_axis(turned[det, :HALO], source, axis=1)
        turned[det, span : span + HALO] = jnp.where(group == groups - 1, 0.0, following)

    for first in range(0, span, CHUNK):
        def direction(number, highest):
            summed = None
            for det in range(dets):
                start = delays_ref[det, number] + first
                term = antenna_ref[det, number] * turned[det, pl.ds(start, CHUNK), :]
                summed = term if summed is None else summed + term
            return jnp.maximum(highest, jnp.abs(summed))

        best[first : first + CHUNK] = lax.fori_loop(
            0, delays_ref.shape[1], direction, jnp.zeros((CHUNK, LANES), jnp.float32), unroll=32
        )
    for near in range(apart):
        back = best[near * LANES : (near + 1) * LANES].T
        for place, group in enumerate(group_at):
            at = (group * apart + near) * LANES
            peak_ref[:, at : at + LANES] = back[place * rows : (place + 1) * rows]


def search(rates, delays, antenna, bank, series, partial, tiles, window, early):
    late, rows, taps = bank.shape
    ready = tiles.shape[0]
    dets = partial.shape[1]
    span = window // (LANES // rows)
    free = pl.BlockSpec(memory_space=pl.ANY)
    vmem = pl.BlockSpec(memory_space=pltpu.VMEM)
    return pl.pallas_call(
        functools.partial(search_kernel, early, ready),
        out_shape=jax.ShapeDtypeStruct((rows, window), jnp.float32),
        in_specs=[free, free, free, vmem, vmem, vmem, vmem],
        out_specs=vmem,
        scratch_shapes=[
            pltpu.SMEM(rates.shape, rates.dtype),
            pltpu.SMEM(delays.shape, delays.dtype),
            pltpu.SMEM(antenna.shape, antenna.dtype),
            pltpu.VMEM(partial.shape[1:], jnp.float32),
            pltpu.VMEM((dets, span + HALO, LANES), jnp.float32),
            pltpu.VMEM((dets, LANES, LANES), jnp.float32),
            pltpu.VMEM((span, LANES), jnp.float32),
            pltpu.SemaphoreType.DMA((3,)),
        ] + [pltpu.VMEM(tiles.shape[1:], tiles.dtype)] * (late > ready),
        compiler_params=pltpu.CompilerParams(vmem_limit_bytes=GRANT),
    )(rates, delays, antenna, bank, series, partial, tiles)


def shards(strain, filters, recon_weights, row_spans, slice_rates, delays, antenna):
    cuts = lax.axis_size("cuts")
    dets = lax.axis_size("det")
    early = min(EARLY, cuts - 2)
    ready = min(READY, cuts - 1 - early)
    bank, series, partial, tiles, rates, delays, antenna = exchange(
        row_spans.reshape(1, -1), strain.reshape(1, -1), filters[0], recon_weights[0],
        slice_rates, delays.T, antenna.T, cuts, dets, early, ready,
    )
    window = strain.shape[-1] - filters.shape[-1]
    return search(rates, delays, antenna, bank, series, partial, tiles, window, early)


def solution(mesh):
    placed = (
        P("cuts", "det", None),
        P(("bank", "cuts"), None, None),
        P(("bank", "cuts"), None, None),
        P("bank"),
        P(),
        P(),
        P(),
    )
    return jax.shard_map(
        shards,
        mesh=mesh,
        in_specs=placed,
        out_specs=P(("bank", "cuts", "det"), None),
        check_vma=False,
    )
```

```python
import functools

import jax
import jax.numpy as jnp
from jax import lax
from jax.experimental import pallas as pl
from jax.experimental.pallas import tpu as pltpu
from jax.sharding import PartitionSpec as P

MESH = pl.DeviceIdType.MESH
LANES = 128
WIDE = 256
DEEP = 48
COARSEST = 8
HALO = 48
CHUNK = 128
EARLY = 2
READY = 1
GRANT = 24 * 2**20


def partner(me, step):
    bit, other = 1, me
    while bit <= step:
        if step & bit:
            other = other + bit * (1 - 2 * lax.rem(lax.div(me, bit), 2))
        bit *= 2
    return other


def tile_count(length):
    return length // LANES


def fill(fetch, tiles, dets, chunks):
    deep = next(deep for deep in range(DEEP, 0, -1) if chunks % deep == 0)
    ahead = lax.broadcasted_iota(jnp.int32, (LANES, LANES), 1) >= lax.broadcasted_iota(
        jnp.int32, (LANES, LANES), 0
    )

    def some(number, carry):
        left = []
        for det, before in zip(dets, carry):
            for near in range(deep):
                chunk = number * deep + near
                piece = fetch(det, pl.multiple_of(chunk * LANES, LANES))
                now = pltpu.roll(jnp.broadcast_to(piece, (LANES, LANES)), 0, 1, stride=1, stride_axis=0)
                tiles[det, chunk] = jnp.where(ahead, now, before).astype(jnp.bfloat16)
                before = now
            left.append(before)
        return tuple(left)

    lax.fori_loop(0, chunks // deep, some, tuple(jnp.zeros((LANES, LANES), jnp.float32) for det in dets))


def stack(bank, pieces):
    taps = bank.astype(jnp.bfloat16)
    return jnp.concatenate([taps[:, piece * WIDE : (piece + 1) * WIDE] for piece in range(pieces)], axis=0)


def convolve(stacked, tiles, dets, pieces, begin, end, blocks, total):
    rows = stacked.shape[0] // pieces
    for det in dets:
        sums = {}
        for near in range(begin, end):
            first = 2 * near + 1
            low, middle, high = tiles[det, first], tiles[det, first + 1], tiles[det, first + 2]
            square = jnp.concatenate(
                [jnp.concatenate([middle, high], axis=1), jnp.concatenate([low, middle], axis=1)], axis=0
            )
            result = jnp.dot(stacked, square, preferred_element_type=jnp.float32)
            for piece in range(pieces):
                block = near + piece - (pieces - 1)
                if 0 <= block < blocks:
                    term = result[piece * rows : (piece + 1) * rows]
                    sums[block] = sums[block] + term if block in sums else term
        for block, value in sums.items():
            for half in range(2):
                at = 2 * block + half
                part = value[:, half * LANES : (half + 1) * LANES]
                total[det, at] = part if begin <= block or not begin else total[det, at] + part


def exchange_kernel(
    cuts, dets, early, ready,
    spans_hbm, strain_hbm, weights_hbm, filters_hbm, rates_hbm, delays_hbm, antenna_hbm,
    bank_ref, series_ref, partial_ref, tiles_ref, rates_ref, delays_ref, antenna_ref,
    spans_ref, strain_ref, weights_ref, filters, bank_stage, bank_early, series, tiles,
    bank_send, bank_recv, cross_send, cross_recv, side_send, side_recv,
    local_sem,
):
    me = lax.axis_index("cuts")
    core = lax.axis_index("det")
    barrier = pltpu.get_barrier_semaphore()
    for step in range(1, cuts):
        pl.semaphore_signal(
            barrier, inc=1, device_id={"cuts": partner(me, step)}, device_id_type=MESH
        )
    for turn in range(1, dets):
        pl.semaphore_signal(
            barrier, inc=1, device_id={"det": lax.rem(core + turn, dets)}, device_id_type=MESH
        )

    fetches = [
        pltpu.make_async_copy(strain_hbm, strain_ref, local_sem.at[0]),
        pltpu.make_async_copy(spans_hbm, spans_ref, local_sem.at[1]),
        pltpu.make_async_copy(weights_hbm, weights_ref, local_sem.at[2]),
        pltpu.make_async_copy(filters_hbm, filters, local_sem.at[3]),
        pltpu.make_async_copy(rates_hbm, rates_ref, local_sem.at[4]),
        pltpu.make_async_copy(delays_hbm, delays_ref, local_sem.at[5]),
        pltpu.make_async_copy(antenna_hbm, antenna_ref, local_sem.at[6]),
    ]
    for copy in fetches:
        copy.start()
    held = early + ready

    def series_at(step, det):
        if step <= held:
            return series.at[step * dets + det]
        return series_ref.at[(step - held - 1) * dets + det]

    def bank_at(step):
        return bank_early.at[step - 1] if step <= early else bank_ref.at[step - early - 1]

    fetches[0].wait()
    series[core] = strain_ref[...].astype(jnp.float32)
    pl.semaphore_wait(barrier, cuts - 1 + dets - 1)
    cross = []
    for step in range(1, cuts):
        cross.append(pltpu.make_async_remote_copy(
            src_ref=series_at(0, core), dst_ref=series_at(step, core),
            send_sem=cross_send.at[step - 1], recv_sem=cross_recv.at[step - 1],
            device_id={"cuts": partner(me, step)}, device_id_type=MESH,
        ))
    side = []
    for step in range(cuts):
        for turn in range(1, dets):
            number = step * (dets - 1) + turn - 1
            side.append(pltpu.make_async_remote_copy(
                src_ref=series_at(step, core), dst_ref=series_at(step, core),
                send_sem=side_send.at[number], recv_sem=side_recv.at[number],
                device_id={"det": lax.rem(core + turn, dets)}, device_id_type=MESH,
            ))
    for copy in cross:
        copy.start()
    for copy in side[: dets - 1]:
        copy.start()

    fetches[1].wait()
    fetches[2].wait()
    rows = weights_ref.shape[0]
    share = rows // cuts // dets
    live = (me < spans_ref[...]).astype(jnp.float32)
    across = lax.broadcasted_iota(jnp.int32, (rows, rows), 1)
    down = lax.broadcasted_iota(jnp.int32, (rows, rows), 0)
    keep = jnp.sum(jnp.where(across == down, live, 0.0), axis=1, keepdims=True)
    kept = (weights_ref[...].astype(jnp.float32) * keep).astype(jnp.bfloat16)
    parts = []
    for cut in range(cuts):
        low = kept[(cut * dets) * share : (cut * dets + 1) * share]
        for det in range(1, dets):
            other = kept[(cut * dets + det) * share : (cut * dets + det + 1) * share]
            low = jnp.where(core == det, other, low)
        parts.append(low)
    stacked = jnp.concatenate(parts, axis=0)
    fetches[3].wait()
    taps = filters.shape[1]
    for first in range(0, taps, WIDE):
        block = jnp.dot(stacked, filters[:, first : first + WIDE], preferred_element_type=jnp.float32)
        for cut in range(cuts):
            bank_stage[cut, :, first : first + WIDE] = block[cut * share : (cut + 1) * share]
    banks = []
    for step in range(1, cuts):
        target = partner(me, step)
        banks.append(pltpu.make_async_remote_copy(
            src_ref=bank_stage.at[target], dst_ref=bank_at(step),
            send_sem=bank_send.at[step - 1], recv_sem=bank_recv.at[step - 1],
            device_id={"cuts": target}, device_id_type=MESH,
        ))
    for copy in banks:
        copy.start()

    pieces = taps // WIDE
    length = series.shape[2]
    window = length - taps
    chunks = length // LANES

    def fetch(step):
        return lambda det, at: series[step * dets + det, :, pl.ds(at, LANES)]

    def filtered(step, bank):
        out = tiles.at[step] if step <= early else tiles_ref.at[step - early - 1]
        coarse = partner(me, step) == cuts - 1

        def work(samples):
            convolve(stack(bank, pieces), out, everyone, pieces, 0, samples // WIDE + pieces - 1, samples // WIDE,
                     partial_ref.at[step])

        pl.when(coarse)(functools.partial(work, window // COARSEST))
        pl.when(jnp.logical_not(coarse))(functools.partial(work, window))

    def prepare(step, det):
        out = tiles.at[step] if step <= early else tiles_ref.at[step - early - 1]
        fill(fetch(step), out, [det], chunks)

    def sides(step):
        return side[step * (dets - 1) : (step + 1) * (dets - 1)]

    def forward(step):
        cross[step - 1].wait_recv()
        for copy in sides(step):
            copy.start()

    def prepare_others(step):
        for copy in sides(step):
            copy.wait_recv()
        for turn in range(1, dets):
            prepare(step, lax.rem(core + turn, dets))

    everyone = list(range(dets))
    prepare(0, core)
    prepare_others(0)
    for step in range(1, early + 1):
        forward(step)
    filtered(0, bank_stage[me])
    for step in range(1, early + 1):
        prepare(step, core)
    for step in range(early + 1, cuts):
        forward(step)
    for step in range(early + 1, held + 1):
        prepare(step, core)
    for step in range(1, held + 1):
        prepare_others(step)
    for step in range(1, early + 1):
        banks[step - 1].wait_recv()
        filtered(step, bank_early[step - 1])
    for copy in fetches[4:]:
        copy.wait()
    for copy in side[(held + 1) * (dets - 1) :]:
        copy.wait_recv()
    for copy in banks[early:]:
        copy.wait_recv()
    for copy in cross + side + banks:
        copy.wait_send()


def exchange(spans, strain, filters, weights, rates, delays, antenna, cuts, dets, early, ready):
    rows = weights.shape[0] // cuts // dets
    taps = filters.shape[1]
    length = strain.shape[-1]
    late = cuts - 1 - early
    rest = max(late - ready, 1)
    hbm = pl.BlockSpec(memory_space=pltpu.HBM)
    free = pl.BlockSpec(memory_space=pl.ANY)
    vmem = pl.BlockSpec(memory_space=pltpu.VMEM)
    dma = pltpu.SemaphoreType.DMA
    squares = (dets, tile_count(length), LANES, LANES)
    return pl.pallas_call(
        functools.partial(exchange_kernel, cuts, dets, early, ready),
        out_shape=(
            jax.ShapeDtypeStruct((late, rows, taps), jnp.float32),
            jax.ShapeDtypeStruct((rest * dets, 1, length), jnp.float32),
            jax.ShapeDtypeStruct((1 + early, dets, (length - taps) // LANES, rows, LANES), jnp.float32),
            jax.ShapeDtypeStruct((ready, *squares), jnp.bfloat16),
            jax.ShapeDtypeStruct(rates.shape, rates.dtype),
            jax.ShapeDtypeStruct(delays.shape, delays.dtype),
            jax.ShapeDtypeStruct(antenna.shape, antenna.dtype),
        ),
        in_specs=[hbm] * 7,
        out_specs=(free, free, vmem, vmem, free, free, free),
        scratch_shapes=[
            pltpu.VMEM(spans.shape, spans.dtype),
            pltpu.VMEM(strain.shape, strain.dtype),
            pltpu.VMEM(weights.shape, weights.dtype),
            pltpu.VMEM(filters.shape, filters.dtype),
            pltpu.VMEM((cuts, rows, taps), jnp.float32),
            pltpu.VMEM((early, rows, taps), jnp.float32),
            pltpu.VMEM(((1 + early + ready) * dets, 1, length), jnp.float32),
            pltpu.VMEM((1 + early, *squares), jnp.bfloat16),
            dma((cuts - 1,)),
            dma((cuts - 1,)),
            dma((cuts - 1,)),
            dma((cuts - 1,)),
            dma((cuts * (dets - 1),)),
            dma((cuts * (dets - 1),)),
            dma((7,)),
        ],
        compiler_params=pltpu.CompilerParams(collective_id=0, has_side_effects=True, vmem_limit_bytes=GRANT),
    )(*[pltpu.with_memory_space_constraint(x, pltpu.HBM)
        for x in (spans, strain, weights, filters, rates, delays, antenna)])


def search_kernel(
    early, ready, rates_any, delays_any, antenna_any, bank_ref, series_ref, partial_ref, tiles_ref, peak_ref,
    rates_ref, delays_ref, antenna_ref, total, turned, best, table_sem, *squares,
):
    tables = [
        pltpu.make_async_copy(rates_any, rates_ref, table_sem.at[0]),
        pltpu.make_async_copy(delays_any, delays_ref, table_sem.at[1]),
        pltpu.make_async_copy(antenna_any, antenna_ref, table_sem.at[2]),
    ]
    for copy in tables:
        copy.start()
    late, rows, taps = bank_ref.shape
    dets = partial_ref.shape[1]
    window = peak_ref.shape[1]
    length = series_ref.shape[2]
    pieces = taps // WIDE
    everyone = list(range(dets))
    me = lax.axis_index("cuts")

    groups = LANES // rows
    apart = window // LANES // groups
    span = apart * LANES
    split = max(1, COARSEST // apart)
    ways = groups // split
    group_at = [place % ways * split + place // ways for place in range(groups)]

    def level_of(step):
        rate = rates_ref[me ^ step]
        return sum((rate >= 2**known).astype(jnp.int32) for known in range(1, COARSEST.bit_length()))

    def widen(values, known, fresh):
        rate = 2**known
        per = apart // rate
        for det in range(dets):
            blocks = []
            for near in range(per):
                block = jnp.concatenate(
                    [values[det, group * per + near] for group in group_at], axis=0
                )
                blocks.append((near * LANES, block.T))
            if not per:
                block = jnp.concatenate([values[det, way] for way in range(ways)], axis=0).T
                part = LANES // split
                blocks = [(0, jnp.concatenate(
                    [block[turn * part : (turn + 1) * part] for turn in range(split)], axis=1
                ))]
            for first, block in blocks:
                size = block.shape[0]
                for turn in range(rate):
                    if rate > 1:
                        place = pl.ds(first * rate + turn, size, stride=rate)
                    else:
                        place = pl.ds(first, size)
                    if fresh:
                        turned[det, place, :] = block
                    else:
                        turned[det, place, :] += block

    def by_level(level, work):
        for known in range(COARSEST.bit_length()):
            pl.when(level == known)(functools.partial(work, known))

    fewest = window // WIDE // COARSEST + pieces - 1

    def begin_slice(index, tiles):
        convolve(stack(bank_ref[index], pieces), tiles, everyone, pieces, 0, fewest, window // WIDE, total)

    def end_slice(index, tiles):
        def work(known):
            blocks = window // WIDE // 2**known
            convolve(
                stack(bank_ref[index], pieces), tiles, everyone, pieces, fewest, blocks + pieces - 1, blocks, total
            )
            widen(total, known, False)

        by_level(level_of(early + 1 + index), work)

    begin_slice(0, tiles_ref.at[0])
    for copy in tables:
        copy.wait()
    for step in range(early + 1):
        by_level(level_of(step), functools.partial(widen, partial_ref.at[step], fresh=step == 0))
    end_slice(0, tiles_ref.at[0])
    for index in range(1, ready):
        begin_slice(index, tiles_ref.at[index])
        end_slice(index, tiles_ref.at[index])
    if late > ready:
        def rest(index, carry):
            fill(
                lambda det, at: series_ref[(index - ready) * dets + det, :, pl.ds(at, LANES)],
                squares[0], everyone, length // LANES,
            )
            begin_slice(index, squares[0])
            end_slice(index, squares[0])
            return carry

        lax.fori_loop(ready, late, rest, 0)

    lane = lax.broadcasted_iota(jnp.int32, (HALO, LANES), 1)
    row, place = lane & (rows - 1), lane // rows
    group = (place & (ways - 1)) * split + place // ways
    later = jnp.minimum(group + 1, groups - 1)
    source = ((later & (split - 1)) * ways + later // split) * rows + row
    for det in range(dets):
        following = jnp.take_along_axis(turned[det, :HALO], source, axis=1)
        turned[det, span : span + HALO] = jnp.where(group == groups - 1, 0.0, following)

    for first in range(0, span, CHUNK):
        def direction(number, highest):
            summed = None
            for det in range(dets):
                start = delays_ref[det, number] + first
                term = antenna_ref[det, number] * turned[det, pl.ds(start, CHUNK), :]
                summed = term if summed is None else summed + term
            return jnp.maximum(highest, jnp.abs(summed))

        best[first : first + CHUNK] = lax.fori_loop(
            0, delays_ref.shape[1], direction, jnp.zeros((CHUNK, LANES), jnp.float32), unroll=16
        )
    for near in range(apart):
        back = best[near * LANES : (near + 1) * LANES].T
        for place, group in enumerate(group_at):
            at = (group * apart + near) * LANES
            peak_ref[:, at : at + LANES] = back[place * rows : (place + 1) * rows]


def search(rates, delays, antenna, bank, series, partial, tiles, window, early):
    late, rows, taps = bank.shape
    ready = tiles.shape[0]
    dets = partial.shape[1]
    span = window // (LANES // rows)
    free = pl.BlockSpec(memory_space=pl.ANY)
    vmem = pl.BlockSpec(memory_space=pltpu.VMEM)
    return pl.pallas_call(
        functools.partial(search_kernel, early, ready),
        out_shape=jax.ShapeDtypeStruct((rows, window), jnp.float32),
        in_specs=[free, free, free, vmem, vmem, vmem, vmem],
        out_specs=vmem,
        scratch_shapes=[
            pltpu.SMEM(rates.shape, rates.dtype),
            pltpu.SMEM(delays.shape, delays.dtype),
            pltpu.SMEM(antenna.shape, antenna.dtype),
            pltpu.VMEM(partial.shape[1:], jnp.float32),
            pltpu.VMEM((dets, span + HALO, LANES), jnp.float32),
            pltpu.VMEM((span, LANES), jnp.float32),
            pltpu.SemaphoreType.DMA((3,)),
        ] + [pltpu.VMEM(tiles.shape[1:], tiles.dtype)] * (late > ready),
        compiler_params=pltpu.CompilerParams(vmem_limit_bytes=GRANT),
    )(rates, delays, antenna, bank, series, partial, tiles)


def shards(strain, filters, recon_weights, row_spans, slice_rates, delays, antenna):
    cuts = lax.axis_size("cuts")
    dets = lax.axis_size("det")
    early = min(EARLY, cuts - 2)
    ready = min(READY, cuts - 1 - early)
    bank, series, partial, tiles, rates, delays, antenna = exchange(
        row_spans.reshape(1, -1), strain.reshape(1, -1), filters[0], recon_weights[0],
        slice_rates, delays.T, antenna.T, cuts, dets, early, ready,
    )
    window = strain.shape[-1] - filters.shape[-1]
    return search(rates, delays, antenna, bank, series, partial, tiles, window, early)


def solution(mesh):
    placed = (
        P("cuts", "det", None),
        P(("bank", "cuts"), None, None),
        P(("bank", "cuts"), None, None),
        P("bank"),
        P(),
        P(),
        P(),
    )
    return jax.shard_map(
        shards,
        mesh=mesh,
        in_specs=placed,
        out_specs=P(("bank", "cuts", "det"), None),
        check_vma=False,
    )
```

```python
import functools

import jax
import jax.numpy as jnp
from jax import lax
from jax.experimental import pallas as pl
from jax.experimental.pallas import tpu as pltpu
from jax.sharding import PartitionSpec as P

MESH = pl.DeviceIdType.MESH
LANES = 128
SUBLANES = 8
WIDE = 256
DEEP = 48
COARSEST = 8
HALO = 48
CHUNK = 64
EARLY = 2
READY = 1
GRANT = 24 * 2**20


def partner(me, step):
    bit, other = 1, me
    while bit <= step:
        if step & bit:
            other = other + bit * (1 - 2 * lax.rem(lax.div(me, bit), 2))
        bit *= 2
    return other


def tile_count(length):
    return length // LANES


def fill(fetch, tiles, dets, chunks):
    deep = next(deep for deep in range(DEEP, 0, -1) if chunks % deep == 0)
    ahead = lax.broadcasted_iota(jnp.int32, (LANES, LANES), 1) >= lax.broadcasted_iota(
        jnp.int32, (LANES, LANES), 0
    )

    def some(number, carry):
        left = []
        for det, before in zip(dets, carry):
            for near in range(deep):
                chunk = number * deep + near
                piece = fetch(det, pl.multiple_of(chunk * LANES, LANES))
                now = pltpu.roll(jnp.broadcast_to(piece, (LANES, LANES)), 0, 1, stride=1, stride_axis=0)
                tiles[det, chunk] = jnp.where(ahead, now, before).astype(jnp.bfloat16)
                before = now
            left.append(before)
        return tuple(left)

    lax.fori_loop(0, chunks // deep, some, tuple(jnp.zeros((LANES, LANES), jnp.float32) for det in dets))


def stack(bank, pieces):
    taps = bank.astype(jnp.bfloat16)
    return jnp.concatenate([taps[:, piece * WIDE : (piece + 1) * WIDE] for piece in range(pieces)], axis=0)


def convolve(stacked, tiles, dets, pieces, begin, end, blocks, total):
    rows = stacked.shape[0] // pieces
    for det in dets:
        sums = {}
        for near in range(begin, end):
            first = 2 * near + 1
            low, middle, high = tiles[det, first], tiles[det, first + 1], tiles[det, first + 2]
            square = jnp.concatenate(
                [jnp.concatenate([middle, high], axis=1), jnp.concatenate([low, middle], axis=1)], axis=0
            )
            result = jnp.dot(stacked, square, preferred_element_type=jnp.float32)
            for piece in range(pieces):
                block = near + piece - (pieces - 1)
                if 0 <= block < blocks:
                    term = result[piece * rows : (piece + 1) * rows]
                    sums[block] = sums[block] + term if block in sums else term
        for block, value in sums.items():
            for half in range(2):
                at = 2 * block + half
                part = value[:, half * LANES : (half + 1) * LANES]
                total[det, at] = part if begin <= block or not begin else total[det, at] + part


def exchange_kernel(
    cuts, dets, early, ready,
    spans_hbm, strain_hbm, weights_hbm, filters_hbm, rates_hbm, delays_hbm, antenna_hbm,
    bank_ref, series_ref, partial_ref, tiles_ref, rates_ref, delays_ref, antenna_ref,
    spans_ref, strain_ref, weights_ref, filters, bank_stage, bank_early, series, tiles,
    bank_send, bank_recv, cross_send, cross_recv, side_send, side_recv,
    local_sem,
):
    me = lax.axis_index("cuts")
    core = lax.axis_index("det")
    barrier = pltpu.get_barrier_semaphore()
    for step in range(1, cuts):
        pl.semaphore_signal(
            barrier, inc=1, device_id={"cuts": partner(me, step)}, device_id_type=MESH
        )
    for turn in range(1, dets):
        pl.semaphore_signal(
            barrier, inc=1, device_id={"det": lax.rem(core + turn, dets)}, device_id_type=MESH
        )

    fetches = [
        pltpu.make_async_copy(strain_hbm, strain_ref, local_sem.at[0]),
        pltpu.make_async_copy(spans_hbm, spans_ref, local_sem.at[1]),
        pltpu.make_async_copy(weights_hbm, weights_ref, local_sem.at[2]),
        pltpu.make_async_copy(filters_hbm, filters, local_sem.at[3]),
        pltpu.make_async_copy(rates_hbm, rates_ref, local_sem.at[4]),
        pltpu.make_async_copy(delays_hbm, delays_ref, local_sem.at[5]),
        pltpu.make_async_copy(antenna_hbm, antenna_ref, local_sem.at[6]),
    ]
    for copy in fetches:
        copy.start()
    held = early + ready

    def series_at(step, det):
        if step <= held:
            return series.at[step * dets + det]
        return series_ref.at[(step - held - 1) * dets + det]

    def bank_at(step):
        return bank_early.at[step - 1] if step <= early else bank_ref.at[step - early - 1]

    fetches[0].wait()
    series[core] = strain_ref[...].astype(jnp.float32)
    pl.semaphore_wait(barrier, cuts - 1 + dets - 1)
    cross = []
    for step in range(1, cuts):
        cross.append(pltpu.make_async_remote_copy(
            src_ref=series_at(0, core), dst_ref=series_at(step, core),
            send_sem=cross_send.at[step - 1], recv_sem=cross_recv.at[step - 1],
            device_id={"cuts": partner(me, step)}, device_id_type=MESH,
        ))
    side = []
    for step in range(cuts):
        for turn in range(1, dets):
            number = step * (dets - 1) + turn - 1
            side.append(pltpu.make_async_remote_copy(
                src_ref=series_at(step, core), dst_ref=series_at(step, core),
                send_sem=side_send.at[number], recv_sem=side_recv.at[number],
                device_id={"det": lax.rem(core + turn, dets)}, device_id_type=MESH,
            ))
    for copy in cross:
        copy.start()
    for copy in side[: dets - 1]:
        copy.start()

    fetches[1].wait()
    fetches[2].wait()
    rows = weights_ref.shape[0]
    share = rows // cuts // dets
    live = (me < spans_ref[...]).astype(jnp.float32)
    across = lax.broadcasted_iota(jnp.int32, (rows, rows), 1)
    down = lax.broadcasted_iota(jnp.int32, (rows, rows), 0)
    keep = jnp.sum(jnp.where(across == down, live, 0.0), axis=1, keepdims=True)
    kept = (weights_ref[...].astype(jnp.float32) * keep).astype(jnp.bfloat16)
    parts = []
    for cut in range(cuts):
        low = kept[(cut * dets) * share : (cut * dets + 1) * share]
        for det in range(1, dets):
            other = kept[(cut * dets + det) * share : (cut * dets + det + 1) * share]
            low = jnp.where(core == det, other, low)
        parts.append(low)
    stacked = jnp.concatenate(parts, axis=0)
    fetches[3].wait()
    taps = filters.shape[1]
    for first in range(0, taps, WIDE):
        block = jnp.dot(stacked, filters[:, first : first + WIDE], preferred_element_type=jnp.float32)
        for cut in range(cuts):
            bank_stage[cut, :, first : first + WIDE] = block[cut * share : (cut + 1) * share]
    banks = []
    for step in range(1, cuts):
        target = partner(me, step)
        banks.append(pltpu.make_async_remote_copy(
            src_ref=bank_stage.at[target], dst_ref=bank_at(step),
            send_sem=bank_send.at[step - 1], recv_sem=bank_recv.at[step - 1],
            device_id={"cuts": target}, device_id_type=MESH,
        ))
    for copy in banks:
        copy.start()

    pieces = taps // WIDE
    length = series.shape[2]
    window = length - taps
    chunks = length // LANES

    def fetch(step):
        return lambda det, at: series[step * dets + det, :, pl.ds(at, LANES)]

    def filtered(step, bank):
        out = tiles.at[step] if step <= early else tiles_ref.at[step - early - 1]
        coarse = partner(me, step) == cuts - 1

        def work(samples):
            convolve(stack(bank, pieces), out, everyone, pieces, 0, samples // WIDE + pieces - 1, samples // WIDE,
                     partial_ref.at[step])

        pl.when(coarse)(functools.partial(work, window // COARSEST))
        pl.when(jnp.logical_not(coarse))(functools.partial(work, window))

    def prepare(step, det):
        out = tiles.at[step] if step <= early else tiles_ref.at[step - early - 1]
        fill(fetch(step), out, [det], chunks)

    def sides(step):
        return side[step * (dets - 1) : (step + 1) * (dets - 1)]

    def forward(step):
        cross[step - 1].wait_recv()
        for copy in sides(step):
            copy.start()

    def prepare_others(step):
        for copy in sides(step):
            copy.wait_recv()
        for turn in range(1, dets):
            prepare(step, lax.rem(core + turn, dets))

    everyone = list(range(dets))
    prepare(0, core)
    prepare_others(0)
    for step in range(1, early + 1):
        forward(step)
    filtered(0, bank_stage[me])
    for step in range(1, early + 1):
        prepare(step, core)
    for step in range(early + 1, cuts):
        forward(step)
    for step in range(early + 1, held + 1):
        prepare(step, core)
    for step in range(1, held + 1):
        prepare_others(step)
    for step in range(1, early + 1):
        banks[step - 1].wait_recv()
        filtered(step, bank_early[step - 1])
    for copy in fetches[4:]:
        copy.wait()
    for copy in side[(held + 1) * (dets - 1) :]:
        copy.wait_recv()
    for copy in banks[early:]:
        copy.wait_recv()
    for copy in cross + side + banks:
        copy.wait_send()


def exchange(spans, strain, filters, weights, rates, delays, antenna, cuts, dets, early, ready):
    rows = weights.shape[0] // cuts // dets
    taps = filters.shape[1]
    length = strain.shape[-1]
    late = cuts - 1 - early
    rest = max(late - ready, 1)
    hbm = pl.BlockSpec(memory_space=pltpu.HBM)
    free = pl.BlockSpec(memory_space=pl.ANY)
    vmem = pl.BlockSpec(memory_space=pltpu.VMEM)
    dma = pltpu.SemaphoreType.DMA
    squares = (dets, tile_count(length), LANES, LANES)
    return pl.pallas_call(
        functools.partial(exchange_kernel, cuts, dets, early, ready),
        out_shape=(
            jax.ShapeDtypeStruct((late, rows, taps), jnp.float32),
            jax.ShapeDtypeStruct((rest * dets, 1, length), jnp.float32),
            jax.ShapeDtypeStruct((1 + early, dets, (length - taps) // LANES, rows, LANES), jnp.float32),
            jax.ShapeDtypeStruct((ready, *squares), jnp.bfloat16),
            jax.ShapeDtypeStruct(rates.shape, rates.dtype),
            jax.ShapeDtypeStruct(delays.shape, delays.dtype),
            jax.ShapeDtypeStruct(antenna.shape, antenna.dtype),
        ),
        in_specs=[hbm] * 7,
        out_specs=(free, free, vmem, vmem, free, free, free),
        scratch_shapes=[
            pltpu.VMEM(spans.shape, spans.dtype),
            pltpu.VMEM(strain.shape, strain.dtype),
            pltpu.VMEM(weights.shape, weights.dtype),
            pltpu.VMEM(filters.shape, filters.dtype),
            pltpu.VMEM((cuts, rows, taps), jnp.float32),
            pltpu.VMEM((early, rows, taps), jnp.float32),
            pltpu.VMEM(((1 + early + ready) * dets, 1, length), jnp.float32),
            pltpu.VMEM((1 + early, *squares), jnp.bfloat16),
            dma((cuts - 1,)),
            dma((cuts - 1,)),
            dma((cuts - 1,)),
            dma((cuts - 1,)),
            dma((cuts * (dets - 1),)),
            dma((cuts * (dets - 1),)),
            dma((7,)),
        ],
        compiler_params=pltpu.CompilerParams(collective_id=0, has_side_effects=True, vmem_limit_bytes=GRANT),
    )(*[pltpu.with_memory_space_constraint(x, pltpu.HBM)
        for x in (spans, strain, weights, filters, rates, delays, antenna)])


def search_kernel(
    early, ready, rates_any, delays_any, antenna_any, bank_ref, series_ref, partial_ref, tiles_ref, peak_ref,
    rates_ref, delays_ref, antenna_ref, total, turned, spread, best, table_sem, *squares,
):
    tables = [
        pltpu.make_async_copy(rates_any, rates_ref, table_sem.at[0]),
        pltpu.make_async_copy(delays_any, delays_ref, table_sem.at[1]),
        pltpu.make_async_copy(antenna_any, antenna_ref, table_sem.at[2]),
    ]
    for copy in tables:
        copy.start()
    late, rows, taps = bank_ref.shape
    dets = partial_ref.shape[1]
    window = peak_ref.shape[1]
    length = series_ref.shape[2]
    pieces = taps // WIDE
    everyone = list(range(dets))
    me = lax.axis_index("cuts")

    groups = LANES // rows
    apart = window // LANES // groups
    span = apart * LANES
    split = max(1, COARSEST // apart)
    ways = groups // split
    group_at = [place % ways * split + place // ways for place in range(groups)]

    def level_of(step):
        rate = rates_ref[me ^ step]
        return sum((rate >= 2**known).astype(jnp.int32) for known in range(1, COARSEST.bit_length()))

    def widen(values, known, fresh):
        rate = 2**known
        per = apart // rate
        for det in range(dets):
            blocks = []
            for near in range(per):
                block = jnp.concatenate(
                    [values[det, group * per + near] for group in group_at], axis=0
                )
                blocks.append((near * LANES, block.T))
            if not per:
                block = jnp.concatenate([values[det, way] for way in range(ways)], axis=0).T
                part = LANES // split
                blocks = [(0, jnp.concatenate(
                    [block[turn * part : (turn + 1) * part] for turn in range(split)], axis=1
                ))]
            for first, block in blocks:
                size = block.shape[0]
                if rate == SUBLANES:
                    spread[det, :size] = block
                    for row in range(size):
                        place = pl.ds((first + row) * rate, rate)
                        value = jnp.broadcast_to(spread[det, row : row + 1], (rate, LANES))
                        turned[det, place, :] = value if fresh else turned[det, place, :] + value
                    continue
                for turn in range(rate):
                    if rate > 1:
                        place = pl.ds(first * rate + turn, size, stride=rate)
                    else:
                        place = pl.ds(first, size)
                    if fresh:
                        turned[det, place, :] = block
                    else:
                        turned[det, place, :] += block

    def by_level(level, work):
        for known in range(COARSEST.bit_length()):
            pl.when(level == known)(functools.partial(work, known))

    fewest = window // WIDE // COARSEST + pieces - 1

    def begin_slice(index, tiles):
        convolve(stack(bank_ref[index], pieces), tiles, everyone, pieces, 0, fewest, window // WIDE, total)

    def end_slice(index, tiles):
        def work(known):
            blocks = window // WIDE // 2**known
            convolve(
                stack(bank_ref[index], pieces), tiles, everyone, pieces, fewest, blocks + pieces - 1, blocks, total
            )
            widen(total, known, False)

        by_level(level_of(early + 1 + index), work)

    begin_slice(0, tiles_ref.at[0])
    for copy in tables:
        copy.wait()
    for step in range(early + 1):
        by_level(level_of(step), functools.partial(widen, partial_ref.at[step], fresh=step == 0))
    end_slice(0, tiles_ref.at[0])
    for index in range(1, ready):
        begin_slice(index, tiles_ref.at[index])
        end_slice(index, tiles_ref.at[index])
    if late > ready:
        def rest(index, carry):
            fill(
                lambda det, at: series_ref[(index - ready) * dets + det, :, pl.ds(at, LANES)],
                squares[0], everyone, length // LANES,
            )
            begin_slice(index, squares[0])
            end_slice(index, squares[0])
            return carry

        lax.fori_loop(ready, late, rest, 0)

    lane = lax.broadcasted_iota(jnp.int32, (HALO, LANES), 1)
    row, place = lane & (rows - 1), lane // rows
    group = (place & (ways - 1)) * split + place // ways
    later = jnp.minimum(group + 1, groups - 1)
    source = ((later & (split - 1)) * ways + later // split) * rows + row
    for det in range(dets):
        following = jnp.take_along_axis(turned[det, :HALO], source, axis=1)
        turned[det, span : span + HALO] = jnp.where(group == groups - 1, 0.0, following)

    for first in range(0, span, CHUNK):
        def direction(number, highest):
            summed = None
            for det in range(dets):
                start = delays_ref[det, number] + first
                term = antenna_ref[det, number] * turned[det, pl.ds(start, CHUNK), :]
                summed = term if summed is None else summed + term
            return jnp.maximum(highest, jnp.abs(summed))

        best[first : first + CHUNK] = lax.fori_loop(
            0, delays_ref.shape[1], direction, jnp.zeros((CHUNK, LANES), jnp.float32), unroll=32
        )
    for near in range(apart):
        back = best[near * LANES : (near + 1) * LANES].T
        for place, group in enumerate(group_at):
            at = (group * apart + near) * LANES
            peak_ref[:, at : at + LANES] = back[place * rows : (place + 1) * rows]


def search(rates, delays, antenna, bank, series, partial, tiles, window, early):
    late, rows, taps = bank.shape
    ready = tiles.shape[0]
    dets = partial.shape[1]
    span = window // (LANES // rows)
    free = pl.BlockSpec(memory_space=pl.ANY)
    vmem = pl.BlockSpec(memory_space=pltpu.VMEM)
    return pl.pallas_call(
        functools.partial(search_kernel, early, ready),
        out_shape=jax.ShapeDtypeStruct((rows, window), jnp.float32),
        in_specs=[free, free, free, vmem, vmem, vmem, vmem],
        out_specs=vmem,
        scratch_shapes=[
            pltpu.SMEM(rates.shape, rates.dtype),
            pltpu.SMEM(delays.shape, delays.dtype),
            pltpu.SMEM(antenna.shape, antenna.dtype),
            pltpu.VMEM(partial.shape[1:], jnp.float32),
            pltpu.VMEM((dets, span + HALO, LANES), jnp.float32),
            pltpu.VMEM((dets, LANES, LANES), jnp.float32),
            pltpu.VMEM((span, LANES), jnp.float32),
            pltpu.SemaphoreType.DMA((3,)),
        ] + [pltpu.VMEM(tiles.shape[1:], tiles.dtype)] * (late > ready),
        compiler_params=pltpu.CompilerParams(vmem_limit_bytes=GRANT),
    )(rates, delays, antenna, bank, series, partial, tiles)


def shards(strain, filters, recon_weights, row_spans, slice_rates, delays, antenna):
    cuts = lax.axis_size("cuts")
    dets = lax.axis_size("det")
    early = min(EARLY, cuts - 2)
    ready = min(READY, cuts - 1 - early)
    bank, series, partial, tiles, rates, delays, antenna = exchange(
        row_spans.reshape(1, -1), strain.reshape(1, -1), filters[0], recon_weights[0],
        slice_rates, delays.T, antenna.T, cuts, dets, early, ready,
    )
    window = strain.shape[-1] - filters.shape[-1]
    return search(rates, delays, antenna, bank, series, partial, tiles, window, early)


def solution(mesh):
    placed = (
        P("cuts", "det", None),
        P(("bank", "cuts"), None, None),
        P(("bank", "cuts"), None, None),
        P("bank"),
        P(),
        P(),
        P(),
    )
    return jax.shard_map(
        shards,
        mesh=mesh,
        in_specs=placed,
        out_specs=P(("bank", "cuts", "det"), None),
        check_vma=False,
    )
```
